256 devices in a mesh: dp: 4 (over y_lo, core), context: 64 (over y_hi, z, x).
Axes of the slice: x: 4, y: 4 (y_hi: 2, y_lo: 2; y = y_hi * 2 + y_lo), z: 8, core: 2. Of those that a mesh axis runs over, the one named last changes fastest.
Arguments:
- queries: bfloat16 [4, 1024, 8192], P('dp', None, 'context'), may hold values from -6 to 6
- key_stream: bfloat16 [4, 1024, 8192], P('dp', None, 'context'), may hold values from -6 to 6
- value_stream: bfloat16 [4, 1024, 8192], P('dp', None, 'context'), may hold values from -6 to 6
- cotangent: bfloat16 [4, 1024, 8192], P('dp', None, 'context'), may hold values from -6 to 6
- short_taps: float32 [3, 3, 1024], replicated, may hold values from -2 to 2
- residues: float32 [1024, 16], P('context'), may hold values from -1.5 to 1.5
- decay_rates: float32 [1024, 16], P('context'), as said below
Outputs:
- output: bfloat16 [4, 1024, 8192], P('dp', None, 'context')
- adjoint_queries: bfloat16 [4, 1024, 8192], P('dp', None, 'context')
- adjoint_keys: bfloat16 [4, 1024, 8192], P('dp', None, 'context')
- adjoint_values: bfloat16 [4, 1024, 8192], P('dp', None, 'context')
- adjoint_taps: float32 [3, 3, 1024], replicated
- adjoint_residues: float32 [1024, 16], P('context')
- adjoint_decays: float32 [1024, 16], P('context')
The draws below stay inside these ranges and needn't reach their ends.
Inputs may be any that keep to these rules, and one draw needn't show every extreme that they name: `decay_rates`: every rate lies between 1 / 16384 and 0.05.
All inputs are finite; a program needn't handle non-finite values.
Results may differ from the reference program's by a relative error of at most 0.017.
Values may be sent and summed in bfloat16 or wider, within the bound.
A program may use at most 128 MiB of HBM per device.

```python
import math
import jax
import jax.numpy as jnp
from jax import lax

CH = 1024
MODES = 16
TAPS = 3
BATCH = 4
LENGTH = 8192


def draw_decay_rates(key, part):
    lowest = jnp.log(0.5 / LENGTH)
    highest = jnp.log(0.05)
    fraction = jax.random.uniform(key, (CH, MODES), jnp.float32)
    return jnp.exp(lowest + (highest - lowest) * fraction)


def block_scale(key, shape, cuts, low, top_value):
    level = 1.0
    for dim, parts in cuts:
        steps = jax.random.uniform(jax.random.fold_in(jax.random.fold_in(key, 6), dim), (parts,), jnp.float32, low / len(cuts), top_value / len(cuts))
        level = level * jnp.repeat(jnp.exp(steps), shape[dim] // parts).reshape((-1,) + (1,) * (len(shape) - 1 - dim))
    return level


def gaussian(key, shape, deviation, most, split=(), held_as=jnp.bfloat16):
    gain = block_scale(key, shape, split, -0.22, 0.18) if split else 1.0
    values = jax.random.normal(key, shape, jnp.float32) * deviation * gain
    return jnp.minimum(jnp.maximum(values, -most), most).astype(held_as)


def setup_inputs(seed: int = 0) -> dict:
    arg_keys = jax.random.split(jax.random.key(seed), 8)
    return {
        "queries": gaussian(arg_keys[0], (BATCH, CH, LENGTH), 1.0, 6.0, ((0, 4), (2, 64))),
        "key_stream": gaussian(arg_keys[1], (BATCH, CH, LENGTH), 1.0, 6.0, ((0, 4), (2, 64))),
        "value_stream": gaussian(arg_keys[2], (BATCH, CH, LENGTH), 1.0, 6.0, ((0, 4), (2, 64))),
        "cotangent": gaussian(arg_keys[3], (BATCH, CH, LENGTH), 1.0, 6.0, ((0, 4), (2, 64))),
        "short_taps": gaussian(arg_keys[4], (3, TAPS, CH), 0.5, 2.0, (), jnp.float32),
        "residues": gaussian(arg_keys[5], (CH, MODES), 0.3, 1.5, ((0, 64),), jnp.float32),
        "decay_rates": draw_decay_rates(jax.random.fold_in(arg_keys[7], 71), 0),
    }


def causal_taps(signal, weights):
    reach_back = weights.shape[0] - 1
    length_here = signal.shape[2]
    padded = jnp.pad(signal, ((0, 0), (0, 0), (reach_back, 0)))
    result = jnp.zeros(signal.shape, signal.dtype)
    for offset in range(reach_back + 1):
        start_at = reach_back - offset
        result = result + weights[offset][None, :, None] * padded[:, :, start_at:start_at + length_here]
    return result

def long_block(inputs):
    source, upstream, residue_block, decay_block = inputs
    seq_length = source.shape[-1]

    def convolve(signal, residue_part, decay_part):
        positions = jnp.arange(seq_length).astype(signal.dtype)
        amplitude = jnp.sqrt(-jnp.expm1(-2.0 * decay_part))
        kernel = jnp.einsum('cm,cmt->ct', residue_part * amplitude, jnp.exp(-decay_part[:, :, None] * positions), precision=lax.Precision.HIGHEST)
        spectrum = jnp.fft.rfft(signal, n=2 * seq_length) * jnp.fft.rfft(kernel, n=2 * seq_length)[None]
        return jnp.fft.irfft(spectrum, n=2 * seq_length)[..., :seq_length]
    mixed_part, pullback = jax.vjp(convolve, source, residue_block, decay_block)
    source_adj, residue_adj, decay_adj = pullback(upstream)
    return (mixed_part, source_adj, residue_adj, decay_adj * decay_block)

def reference(queries, key_stream, value_stream, cotangent, short_taps, residues, decay_rates):
    batch_count, channels, seq_length = queries.shape
    mode_count = residues.shape[1]
    featured = []
    pullers = []
    for stream, signal in enumerate((queries, key_stream, value_stream)):
        shaped, puller = jax.vjp(causal_taps, signal.astype(jnp.float32), short_taps[stream])
        featured.append(shaped.astype(jnp.bfloat16))
        pullers.append(puller)
    query_short, key_short, value_short = featured
    gated = (key_short.astype(jnp.float32) * value_short.astype(jnp.float32)).astype(jnp.bfloat16)
    upstream = (cotangent.astype(jnp.float32) * query_short.astype(jnp.float32)).astype(jnp.bfloat16)
    block_width = min(64, channels)
    blocks = channels // block_width

    def split_blocks(array):
        return array.reshape(batch_count, blocks, block_width, seq_length).transpose(1, 0, 2, 3)

    def join_blocks(array):
        return array.transpose(1, 0, 2, 3).reshape(batch_count, channels, seq_length)
    mixed_all, source_all, residue_adj, decay_adj = lax.map(long_block, (split_blocks(gated.astype(jnp.float32)), split_blocks(upstream.astype(jnp.float32)), residues.reshape(blocks, block_width, mode_count), decay_rates.reshape(blocks, block_width, mode_count)))
    mixed = join_blocks(mixed_all).astype(jnp.bfloat16)
    output = (query_short.astype(jnp.float32) * mixed.astype(jnp.float32)).astype(jnp.bfloat16)
    source_low = join_blocks(source_all).astype(jnp.bfloat16)
    query_adj = (cotangent.astype(jnp.float32) * mixed.astype(jnp.float32)).astype(jnp.bfloat16)
    key_adj = (source_low.astype(jnp.float32) * value_short.astype(jnp.float32)).astype(jnp.bfloat16)
    value_adj = (source_low.astype(jnp.float32) * key_short.astype(jnp.float32)).astype(jnp.bfloat16)
    adjoints = []
    tap_terms = []
    for puller, adjoint in zip(pullers, (query_adj, key_adj, value_adj)):
        signal_adj, taps_adj = puller(adjoint.astype(jnp.float32))
        adjoints.append(signal_adj.astype(jnp.bfloat16))
        tap_terms.append(taps_adj)
    token_scale = 1.0 / math.sqrt(batch_count * seq_length)
    return (output, adjoints[0], adjoints[1], adjoints[2], jnp.stack(tap_terms) * token_scale, residue_adj.reshape(channels, mode_count) * token_scale, decay_adj.reshape(channels, mode_count) * token_scale)
```

```python
import functools
import math

import jax
import jax.numpy as jnp
from jax import lax
from jax.experimental import pallas as pl
from jax.experimental.pallas import tpu as pltpu
from jax.sharding import PartitionSpec as P

F32 = jnp.float32
BF16 = jnp.bfloat16
HIGHEST = lax.Precision.HIGHEST
LANES = 128
SUBS = 8
GROUP = 8


def rounded(x):
    return x.astype(BF16).astype(F32)


def owner_kernel(
    own, modes, taps, steps, scale,
    q_ref, k_ref, v_ref, c_ref, table_ref,
    out_ref, dq_ref, dk_ref, dv_ref, small_ref,
    xq, xk, xv, xc, qs, ks, vs, gs, us, ys, ss, aq, ak, av,
    tab, lst, pst, adj, qacc, racc, tacc,
):
    lane = lax.broadcasted_iota(jnp.int32, (SUBS, LANES), 1)
    sub = lax.broadcasted_iota(jnp.int32, (SUBS, LANES), 0)
    per_row = LANES // own
    chunk = sub * per_row + lane // own
    chunks = SUBS * per_row

    def later(x, by):
        if by < per_row:
            turned = pltpu.roll(x, own * by, 1)
            x = jnp.where(lane >= own * by, turned, pltpu.roll(turned, 1, 0))
        else:
            x = pltpu.roll(x, by // per_row, 0)
        return jnp.where(chunk >= by, x, 0.0)

    def earlier(x, by):
        if by < per_row:
            turned = pltpu.roll(x, LANES - own * by, 1)
            x = jnp.where(lane < LANES - own * by, turned, pltpu.roll(turned, SUBS - 1, 0))
        else:
            x = pltpu.roll(x, SUBS - by // per_row, 0)
        return jnp.where(chunk < chunks - by, x, 0.0)

    def at(t):
        return pl.ds(pl.multiple_of(t * SUBS, SUBS), SUBS)

    spread = (
        lax.broadcasted_iota(jnp.int32, (own, LANES), 0)
        == lax.broadcasted_iota(jnp.int32, (own, LANES), 1) % own
    ).astype(F32)
    rows = jnp.dot(table_ref[...], spread, precision=HIGHEST, preferred_element_type=F32)
    n_rows = 3 * modes + 3 * taps
    for row in range(n_rows):
        tab[pl.ds(row * SUBS, SUBS), :] = jnp.broadcast_to(rows[row : row + 1, :], (SUBS, LANES))

    def entry(row):
        return tab[pl.ds(row * SUBS, SUBS), :]

    ones = (
        lax.broadcasted_iota(jnp.int32, (LANES, LANES), 0)
        == lax.broadcasted_iota(jnp.int32, (LANES, LANES), 1)
    ).astype(BF16)

    def flipped(x):
        return lax.dot_general(ones, x, (((1,), (1,)), ((), ())), preferred_element_type=F32)

    reach = taps - 1
    head = reach * SUBS
    for src, dst in ((q_ref, xq), (k_ref, xk), (v_ref, xv), (c_ref, xc)):
        for i in range(SUBS):
            dst[pl.ds(head + i, steps, stride=SUBS), :] = flipped(src[pl.ds(i * LANES, LANES), :])
    for x in (xq, xk, xv):
        for j in range(reach):
            x[pl.ds(j * SUBS, SUBS), :] = later(x[pl.ds(head + (steps - reach + j) * SUBS, SUBS), :], 1)

    def tap(stream, j):
        return entry(3 * modes + stream * taps + j)

    def filtered(x, stream, t):
        total = tap(stream, 0) * x[at(t + reach), :]
        for j in range(1, taps):
            total = total + tap(stream, j) * x[at(t + reach - j), :]
        return rounded(total)

    def features(t, carry):
        query, key, value = filtered(xq, 0, t), filtered(xk, 1, t), filtered(xv, 2, t)
        qs[at(t), :] = query
        ks[at(t), :] = key
        vs[at(t), :] = value
        gs[at(t), :] = rounded(key * value)
        us[at(t), :] = rounded(xc[at(t + reach), :] * query)
        return carry

    lax.fori_loop(0, steps, features, 0, unroll=4)

    zero = jnp.zeros((SUBS, LANES), F32)

    def ends(t, carry):
        gated = gs[at(t), :]
        upstream = us[at(steps - 1 - t), :]
        ahead, back = carry
        decays = [entry(m) for m in range(modes)]
        return (
            tuple(decays[m] * ahead[m] + gated for m in range(modes)),
            tuple(decays[m] * back[m] + upstream for m in range(modes)),
        )

    zeros = tuple(zero for _ in range(modes))
    ahead, back = lax.fori_loop(0, steps, ends, (zeros, zeros), unroll=2)
    for m in range(modes):
        lst[pl.ds(m * SUBS, SUBS), :] = ahead[m]
        pst[pl.ds(m * SUBS, SUBS), :] = back[m]

    def chain(m, carry):
        power = tab[at(m + n_rows), :]
        total, behind = lst[at(m), :], pst[at(m), :]
        by = 1
        while by < chunks:
            total = total + power * later(total, by)
            behind = behind + power * earlier(behind, by)
            power = power * power
            by *= 2
        lst[at(m), :] = later(total, 1)
        pst[at(m), :] = earlier(behind, 1)
        return carry

    for m in range(modes):
        decay = entry(modes + m)
        tab[pl.ds((n_rows + m) * SUBS, SUBS), :] = jnp.exp(decay * (-float(steps)))
    lax.fori_loop(0, modes, chain, 0)

    for group in range(0, modes, GROUP):
        members = range(group, group + GROUP)

        def backward(i, carry):
            t = steps - 1 - i
            upstream = us[at(t), :]
            total = zero if group == 0 else ss[at(t), :]
            new = []
            for n, m in enumerate(members):
                state = entry(m) * carry[n] + upstream
                adj[at(t * GROUP + n), :] = state
                total = total + entry(2 * modes + m) * state
                new.append(state)
            ss[at(t), :] = total
            return tuple(new)

        lax.fori_loop(0, steps, backward, tuple(pst[pl.ds(m * SUBS, SUBS), :] for m in members), unroll=2)

        def forward(t, carry):
            states, firsts, seconds = carry
            gated = gs[at(t), :]
            upstream = us[at(t), :]
            total = zero if group == 0 else ys[at(t), :]
            new_s, new_f, new_r = [], [], []
            for n, m in enumerate(members):
                new_r.append(seconds[n] + states[n] * adj[at(t * GROUP + n), :])
                state = entry(m) * states[n] + gated
                new_f.append(firsts[n] + upstream * state)
                total = total + entry(2 * modes + m) * state
                new_s.append(state)
            ys[at(t), :] = total
            return tuple(new_s), tuple(new_f), tuple(new_r)

        few = tuple(zero for _ in members)
        _, firsts, seconds = lax.fori_loop(
            0, steps, forward, (tuple(lst[pl.ds(m * SUBS, SUBS), :] for m in members), few, few), unroll=2
        )
        for n, m in enumerate(members):
            qacc[pl.ds(m, 1), :] = jnp.sum(firsts[n], axis=0, keepdims=True)
            racc[pl.ds(m, 1), :] = jnp.sum(seconds[n], axis=0, keepdims=True)

    def products(t, carry):
        mixed = rounded(ys[at(t), :])
        source = rounded(ss[at(t), :])
        query = qs[at(t), :]
        ys[at(t), :] = query * mixed
        grads = (
            rounded(xc[at(t + reach), :] * mixed),
            rounded(source * vs[at(t), :]),
            rounded(source * ks[at(t), :]),
        )
        new = []
        for stream, (grad, ref, x) in enumerate(zip(grads, (aq, ak, av), (xq, xk, xv))):
            ref[at(t), :] = grad
            for j in range(taps):
                new.append(carry[stream * taps + j] + grad * x[at(t + reach - j), :])
        return tuple(new)

    tacc[...] = jnp.zeros(tacc.shape, F32)
    sums = lax.fori_loop(0, steps, products, tuple(zero for _ in range(3 * taps)), unroll=2)
    for n in range(3 * taps):
        tacc[pl.ds(n, 1), :] = jnp.sum(sums[n], axis=0, keepdims=True)

    for a in (aq, ak, av):
        for j in range(reach):
            a[pl.ds((steps + j) * SUBS, SUBS), :] = earlier(a[pl.ds(j * SUBS, SUBS), :], 1)

    def gradients(t, carry):
        for stream, (a, dst) in enumerate(((aq, gs), (ak, us), (av, ss))):
            total = tap(stream, 0) * a[at(t), :]
            for j in range(1, taps):
                total = total + tap(stream, j) * a[at(t + j), :]
            dst[at(t), :] = total
        return carry

    lax.fori_loop(0, steps, gradients, 0, unroll=4)
    for src, dst in ((ys, out_ref), (gs, dq_ref), (us, dk_ref), (ss, dv_ref)):
        for i in range(SUBS):
            part = src[pl.ds(i, steps, stride=SUBS), :].astype(BF16)
            dst[pl.ds(i * LANES, LANES), :] = flipped(part).astype(BF16)

    def over_chunks(x):
        by = own
        while by < LANES:
            x = x + pltpu.roll(x, by, 1)
            by *= 2
        return x

    first = over_chunks(qacc[...])
    second = over_chunks(racc[...]) * rows[:modes]
    decay = rows[modes : 2 * modes]
    weighted = rows[2 * modes : 3 * modes]
    size = table_sizes(table_ref, n_rows, modes, spread)
    damp = rows[:modes] * rows[:modes]
    small_ref[pl.ds(0, modes), :] = scale * size * first
    bend = residue_part(table_ref, n_rows, modes, spread) * (damp / size) * first - weighted * second
    small_ref[pl.ds(modes, modes), :] = scale * decay * bend
    small_ref[pl.ds(2 * modes, tacc.shape[0]), :] = scale * over_chunks(tacc[...])


def table_sizes(table_ref, start, modes, spread):
    part = table_ref[pl.ds(TABLE_EXTRA, modes), :]
    return jnp.dot(part, spread, precision=HIGHEST, preferred_element_type=F32)


def residue_part(table_ref, start, modes, spread):
    part = table_ref[pl.ds(TABLE_EXTRA + modes, modes), :]
    return jnp.dot(part, spread, precision=HIGHEST, preferred_element_type=F32)


TABLE_EXTRA = 64


def per_device(queries, key_stream, value_stream, cotangent, short_taps, residues, decay_rates):
    channels, steps = queries.shape[1], queries.shape[2]
    own, modes = residues.shape
    taps = short_taps.shape[1]
    owners = lax.axis_size("context")
    scale = 1.0 / math.sqrt(queries.shape[0] * lax.axis_size("dp") * steps * owners)
    me = lax.axis_index("context")

    mine = [
        lax.all_to_all(x.reshape(channels, steps), "context", 0, 0, tiled=True)
        for x in (queries, key_stream, value_stream, cotangent)
    ]
    rates = decay_rates.T
    size = jnp.sqrt(-jnp.expm1(-2.0 * rates))
    own_taps = lax.dynamic_slice(short_taps.reshape(3 * taps, channels), (0, me * own), (3 * taps, own))
    n_rows = 3 * modes + 3 * taps
    table = jnp.concatenate(
        [
            jnp.exp(-rates),
            rates,
            residues.T * size,
            own_taps,
            jnp.zeros((TABLE_EXTRA - n_rows, own), F32),
            size,
            residues.T,
        ]
    )
    wide = jax.ShapeDtypeStruct((channels, steps), BF16)
    line = steps * SUBS
    reach = taps - 1
    vm = pltpu.VMEM
    tap_rows = 16
    results = pl.pallas_call(
        functools.partial(owner_kernel, own, modes, taps, steps, scale),
        out_shape=[wide] * 4 + [jax.ShapeDtypeStruct((2 * modes + tap_rows, LANES), F32)],
        in_specs=[pl.BlockSpec(memory_space=vm)] * 5,
        out_specs=[pl.BlockSpec(memory_space=vm)] * 5,
        scratch_shapes=[vm((line + reach * SUBS, LANES), F32)] * 4
        + [vm((line, LANES), F32)] * 7
        + [vm((line + reach * SUBS, LANES), F32)] * 3
        + [
            vm(((n_rows + modes) * SUBS, LANES), F32),
            vm((modes * SUBS, LANES), F32),
            vm((modes * SUBS, LANES), F32),
            vm((line * GROUP, LANES), F32),
            vm((modes, LANES), F32),
            vm((modes, LANES), F32),
            vm((tap_rows, LANES), F32),
        ],
        compiler_params=pltpu.CompilerParams(vmem_limit_bytes=48 * 1024 * 1024),
    )(*mine, table)
    small = results[4][:, :own]
    for by in (1, 2):
        small = small + lax.ppermute(small, "dp", [(i, i ^ by) for i in range(lax.axis_size("dp"))])
    outs = [
        lax.all_to_all(x, "context", 0, 0, tiled=True).reshape(queries.shape) for x in results[:4]
    ]
    flat = jnp.pad(small[2 * modes : 2 * modes + 3 * taps].reshape(-1), (0, 2 * LANES - 3 * taps * own))
    shared = lax.all_to_all(
        jnp.broadcast_to(flat.reshape(1, 2, LANES), (owners, 2, LANES)), "context", 0, 0, tiled=True
    )
    tap_total = shared.reshape(owners, 2 * LANES)[:, : 3 * taps * own].reshape(owners, 3, taps, own)
    tap_total = tap_total.transpose(1, 2, 0, 3).reshape(3, taps, channels)
    return (*outs, tap_total, small[:modes].T, small[modes : 2 * modes].T)


def solution(mesh):
    stream = P("dp", None, "context")
    in_specs = (stream,) * 4 + (P(), P("context", None), P("context", None))
    out_specs = (stream,) * 4 + (P(), P("context", None), P("context", None))
    return jax.shard_map(per_device, mesh=mesh, in_specs=in_specs, out_specs=out_specs, check_vma=False)
```

```python
import functools
import math

import jax
import jax.numpy as jnp
from jax import lax
from jax.experimental import pallas as pl
from jax.experimental.pallas import tpu as pltpu
from jax.sharding import PartitionSpec as P

F32 = jnp.float32
BF16 = jnp.bfloat16
HIGHEST = lax.Precision.HIGHEST
LANES = 128
SUBS = 8
GROUP = 8


def rounded(x):
    return x.astype(BF16).astype(F32)


def owner_kernel(
    own, modes, taps, steps, scale,
    q_ref, k_ref, v_ref, c_ref, table_ref,
    out_ref, dq_ref, dk_ref, dv_ref, small_ref,
    xq, xk, xv, xc, qs, ks, vs, gs, us, ys, ss, aq, ak, av,
    tab, lst, pst, adj, qacc, racc, tacc,
):
    lane = lax.broadcasted_iota(jnp.int32, (SUBS, LANES), 1)
    sub = lax.broadcasted_iota(jnp.int32, (SUBS, LANES), 0)
    per_row = LANES // own
    chunk = sub * per_row + lane // own
    chunks = SUBS * per_row

    def later(x, by):
        if by < per_row:
            turned = pltpu.roll(x, own * by, 1)
            x = jnp.where(lane >= own * by, turned, pltpu.roll(turned, 1, 0))
        else:
            x = pltpu.roll(x, by // per_row, 0)
        return jnp.where(chunk >= by, x, 0.0)

    def earlier(x, by):
        if by < per_row:
            turned = pltpu.roll(x, LANES - own * by, 1)
            x = jnp.where(lane < LANES - own * by, turned, pltpu.roll(turned, SUBS - 1, 0))
        else:
            x = pltpu.roll(x, SUBS - by // per_row, 0)
        return jnp.where(chunk < chunks - by, x, 0.0)

    def at(t):
        return pl.ds(pl.multiple_of(t * SUBS, SUBS), SUBS)

    spread = (
        lax.broadcasted_iota(jnp.int32, (own, LANES), 0)
        == lax.broadcasted_iota(jnp.int32, (own, LANES), 1) % own
    ).astype(F32)
    rows = jnp.dot(table_ref[...], spread, precision=HIGHEST, preferred_element_type=F32)
    n_rows = 3 * modes + 3 * taps
    for row in range(n_rows):
        tab[pl.ds(row * SUBS, SUBS), :] = jnp.broadcast_to(rows[row : row + 1, :], (SUBS, LANES))

    def entry(row):
        return tab[pl.ds(row * SUBS, SUBS), :]

    ones = (
        lax.broadcasted_iota(jnp.int32, (LANES, LANES), 0)
        == lax.broadcasted_iota(jnp.int32, (LANES, LANES), 1)
    ).astype(BF16)

    def flipped(x):
        return lax.dot_general(ones, x, (((1,), (1,)), ((), ())), preferred_element_type=F32)

    reach = taps - 1
    head = reach * SUBS
    for src, dst in ((q_ref, xq), (k_ref, xk), (v_ref, xv), (c_ref, xc)):
        for i in range(SUBS):
            dst[pl.ds(head + i, steps, stride=SUBS), :] = flipped(src[pl.ds(i * LANES, LANES), :])
    for x in (xq, xk, xv):
        for j in range(reach):
            x[pl.ds(j * SUBS, SUBS), :] = later(x[pl.ds(head + (steps - reach + j) * SUBS, SUBS), :], 1)

    def tap(stream, j):
        return entry(3 * modes + stream * taps + j)

    def filtered(x, stream, t):
        total = tap(stream, 0) * x[at(t + reach), :]
        for j in range(1, taps):
            total = total + tap(stream, j) * x[at(t + reach - j), :]
        return rounded(total)

    def features(t, carry):
        query, key, value = filtered(xq, 0, t), filtered(xk, 1, t), filtered(xv, 2, t)
        qs[at(t), :] = query
        ks[at(t), :] = key
        vs[at(t), :] = value
        gs[at(t), :] = rounded(key * value)
        us[at(t), :] = rounded(xc[at(t + reach), :] * query)
        return carry

    lax.fori_loop(0, steps, features, 0, unroll=4)

    zero = jnp.zeros((SUBS, LANES), F32)

    def ends(t, carry):
        gated = gs[at(t), :]
        upstream = us[at(steps - 1 - t), :]
        ahead, back = carry
        decays = [entry(m) for m in range(modes)]
        return (
            tuple(decays[m] * ahead[m] + gated for m in range(modes)),
            tuple(decays[m] * back[m] + upstream for m in range(modes)),
        )

    zeros = tuple(zero for _ in range(modes))
    ahead, back = lax.fori_loop(0, steps, ends, (zeros, zeros), unroll=2)
    for m in range(modes):
        lst[pl.ds(m * SUBS, SUBS), :] = ahead[m]
        pst[pl.ds(m * SUBS, SUBS), :] = back[m]

    def chain(m, carry):
        power = tab[at(m + n_rows), :]
        total, behind = lst[at(m), :], pst[at(m), :]
        by = 1
        while by < chunks:
            total = total + power * later(total, by)
            behind = behind + power * earlier(behind, by)
            power = power * power
            by *= 2
        lst[at(m), :] = later(total, 1)
        pst[at(m), :] = earlier(behind, 1)
        return carry

    for m in range(modes):
        decay = entry(modes + m)
        tab[pl.ds((n_rows + m) * SUBS, SUBS), :] = jnp.exp(decay * (-float(steps)))
    lax.fori_loop(0, modes, chain, 0)

    for group in range(0, modes, GROUP):
        members = range(group, group + GROUP)

        def backward(i, carry):
            t = steps - 1 - i
            upstream = us[at(t), :]
            total = zero if group == 0 else ss[at(t), :]
            new = []
            for n, m in enumerate(members):
                state = entry(m) * carry[n] + upstream
                adj[at(t * GROUP + n), :] = state
                total = total + entry(2 * modes + m) * state
                new.append(state)
            ss[at(t), :] = total
            return tuple(new)

        lax.fori_loop(0, steps, backward, tuple(pst[pl.ds(m * SUBS, SUBS), :] for m in members), unroll=2)

        def forward(t, carry):
            states, firsts, seconds = carry
            gated = gs[at(t), :]
            upstream = us[at(t), :]
            total = zero if group == 0 else ys[at(t), :]
            new_s, new_f, new_r = [], [], []
            for n, m in enumerate(members):
                new_r.append(seconds[n] + states[n] * adj[at(t * GROUP + n), :])
                state = entry(m) * states[n] + gated
                new_f.append(firsts[n] + upstream * state)
                total = total + entry(2 * modes + m) * state
                new_s.append(state)
            ys[at(t), :] = total
            return tuple(new_s), tuple(new_f), tuple(new_r)

        few = tuple(zero for _ in members)
        _, firsts, seconds = lax.fori_loop(
            0, steps, forward, (tuple(lst[pl.ds(m * SUBS, SUBS), :] for m in members), few, few), unroll=2
        )
        for n, m in enumerate(members):
            qacc[pl.ds(m, 1), :] = jnp.sum(firsts[n], axis=0, keepdims=True)
            racc[pl.ds(m, 1), :] = jnp.sum(seconds[n], axis=0, keepdims=True)

    def products(t, carry):
        mixed = rounded(ys[at(t), :])
        source = rounded(ss[at(t), :])
        query = qs[at(t), :]
        ys[at(t), :] = query * mixed
        grads = (
            rounded(xc[at(t + reach), :] * mixed),
            rounded(source * vs[at(t), :]),
            rounded(source * ks[at(t), :]),
        )
        new = []
        for stream, (grad, ref, x) in enumerate(zip(grads, (aq, ak, av), (xq, xk, xv))):
            ref[at(t), :] = grad
            for j in range(taps):
                new.append(carry[stream * taps + j] + grad * x[at(t + reach - j), :])
        return tuple(new)

    tacc[...] = jnp.zeros(tacc.shape, F32)
    sums = lax.fori_loop(0, steps, products, tuple(zero for _ in range(3 * taps)), unroll=2)
    for n in range(3 * taps):
        tacc[pl.ds(n, 1), :] = jnp.sum(sums[n], axis=0, keepdims=True)

    for a in (aq, ak, av):
        for j in range(reach):
            a[pl.ds((steps + j) * SUBS, SUBS), :] = earlier(a[pl.ds(j * SUBS, SUBS), :], 1)

    def gradients(t, carry):
        for stream, (a, dst) in enumerate(((aq, gs), (ak, us), (av, ss))):
            total = tap(stream, 0) * a[at(t), :]
            for j in range(1, taps):
                total = total + tap(stream, j) * a[at(t + j), :]
            dst[at(t), :] = total
        return carry

    lax.fori_loop(0, steps, gradients, 0, unroll=4)
    for src, dst in ((ys, out_ref), (gs, dq_ref), (us, dk_ref), (ss, dv_ref)):
        for i in range(SUBS):
            part = src[pl.ds(i, steps, stride=SUBS), :].astype(BF16)
            dst[pl.ds(i * LANES, LANES), :] = flipped(part).astype(BF16)

    def over_chunks(x):
        by = own
        while by < LANES:
            x = x + pltpu.roll(x, by, 1)
            by *= 2
        return x

    first = over_chunks(qacc[...])
    second = over_chunks(racc[...]) * rows[:modes]
    decay = rows[modes : 2 * modes]
    weighted = rows[2 * modes : 3 * modes]
    size = table_sizes(table_ref, n_rows, modes, spread)
    damp = rows[:modes] * rows[:modes]
    small_ref[pl.ds(0, modes), :] = scale * size * first
    bend = residue_part(table_ref, n_rows, modes, spread) * (damp / size) * first - weighted * second
    small_ref[pl.ds(modes, modes), :] = scale * decay * bend
    total_taps = scale * over_chunks(tacc[...])
    part = lax.broadcasted_iota(jnp.int32, (1, LANES), 1) // own
    packed = jnp.zeros((SUBS, LANES), F32)
    for n in range(3 * taps):
        spot = (part == n % per_row) & (sub == n // per_row)
        packed = jnp.where(spot, total_taps[n : n + 1, :], packed)
    small_ref[pl.ds(2 * modes, SUBS), :] = packed


def table_sizes(table_ref, start, modes, spread):
    part = table_ref[pl.ds(TABLE_EXTRA, modes), :]
    return jnp.dot(part, spread, precision=HIGHEST, preferred_element_type=F32)


def residue_part(table_ref, start, modes, spread):
    part = table_ref[pl.ds(TABLE_EXTRA + modes, modes), :]
    return jnp.dot(part, spread, precision=HIGHEST, preferred_element_type=F32)


TABLE_EXTRA = 64


MESH = pl.DeviceIdType.MESH


def greet(axis, peers, me):
    barrier = pltpu.get_barrier_semaphore()

    def signal(step, carry):
        pl.semaphore_signal(barrier, inc=1, device_id={axis: lax.rem(me + step, peers)}, device_id_type=MESH)
        return carry

    lax.fori_loop(1, peers, signal, 0)
    return barrier


def exchange(own, peers, me, sources, targets, send_sem, recv_sem):
    def piece(i):
        return pl.ds(pl.multiple_of(i * own, own), own)

    def send(step, carry):
        peer = lax.rem(me + step, peers)
        for n, (source, target) in enumerate(zip(sources, targets)):
            pltpu.make_async_remote_copy(
                src_ref=source.at[piece(peer)],
                dst_ref=target.at[piece(me)],
                send_sem=send_sem.at[n],
                recv_sem=recv_sem.at[n],
                device_id={"context": peer},
                device_id_type=MESH,
            ).start()
        return carry

    lax.fori_loop(1, peers, send, 0)


def settle(rows, refs, sem):
    for n, ref in enumerate(refs):
        whole = ref.at[pl.ds(0, rows)]
        pltpu.make_async_copy(whole, whole, sem.at[n]).wait()


def keep(own, me, sources, targets, sem):
    spot = pl.ds(pl.multiple_of(me * own, own), own)
    copies = [
        pltpu.make_async_copy(source.at[spot], target.at[spot], sem.at[n])
        for n, (source, target) in enumerate(zip(sources, targets))
    ]
    for copy in copies:
        copy.start()
    return copies


def inbound_kernel(own, peers, *refs):
    sources, targets = refs[:4], refs[4:8]
    send_sem, recv_sem, keep_sem = refs[8:]
    me = lax.axis_index("context")
    barrier = greet("context", peers, me)
    copies = keep(own, me, sources, targets, keep_sem)
    pl.semaphore_wait(barrier, peers - 1)
    exchange(own, peers, me, sources, targets, send_sem, recv_sem)
    for copy in copies:
        copy.wait()
    settle(own * (peers - 1), targets, recv_sem)
    settle(own * (peers - 1), sources, send_sem)


def outbound_kernel(own, peers, doubles, rows, used, *refs):
    sources, small, targets, total, shared = refs[:4], refs[4], refs[5:9], refs[9], refs[10]
    slots, send_sem, recv_sem, keep_sem, pair_send, pair_recv, tap_send, tap_recv = refs[11:]
    me = lax.axis_index("context")
    mine = lax.axis_index("dp")
    barrier = greet("context", peers, me)
    greet("dp", doubles, mine)
    copies = keep(own, me, sources, targets, keep_sem)
    own_small = pltpu.make_async_copy(small, slots.at[mine], keep_sem.at[4])
    own_small.start()
    pl.semaphore_wait(barrier, peers + doubles - 2)
    pairs = []
    for step in range(1, doubles):
        pairs.append(
            pltpu.make_async_remote_copy(
                src_ref=small,
                dst_ref=slots.at[mine],
                send_sem=pair_send.at[step],
                recv_sem=pair_recv.at[step],
                device_id={"dp": lax.rem(mine + step, doubles)},
                device_id_type=MESH,
            )
        )
    for pair in pairs:
        pair.start()
    exchange(own, peers, me, sources, targets, send_sem, recv_sem)
    own_small.wait()
    for pair in pairs:
        pair.wait()
    total[...] = (slots[0] + slots[1]) + (slots[2] + slots[3])
    spot = pl.ds(pl.multiple_of(me * SUBS, SUBS), used)
    taps = total.at[pl.ds(rows, used)]
    own_taps = pltpu.make_async_copy(taps, shared.at[spot], keep_sem.at[5])
    own_taps.start()

    def send(step, carry):
        pltpu.make_async_remote_copy(
            src_ref=taps,
            dst_ref=shared.at[spot],
            send_sem=tap_send,
            recv_sem=tap_recv,
            device_id={"context": lax.rem(me + step, peers)},
            device_id_type=MESH,
        ).start()
        return carry

    lax.fori_loop(1, peers, send, 0)
    for copy in copies:
        copy.wait()
    own_taps.wait()
    settle(own * (peers - 1), targets, recv_sem)
    settle(own * (peers - 1), sources, send_sem)
    whole = shared.at[pl.ds(0, used * (peers - 1))]
    pltpu.make_async_copy(whole, whole, tap_recv).wait()
    pltpu.make_async_copy(whole, whole, tap_send).wait()


def per_device(queries, key_stream, value_stream, cotangent, short_taps, residues, decay_rates):
    channels, steps = queries.shape[1], queries.shape[2]
    own, modes = residues.shape
    taps = short_taps.shape[1]
    owners = lax.axis_size("context")
    scale = 1.0 / math.sqrt(queries.shape[0] * lax.axis_size("dp") * steps * owners)
    me = lax.axis_index("context")

    wide = jax.ShapeDtypeStruct((channels, steps), BF16)
    vm = pltpu.VMEM
    here = pl.BlockSpec(memory_space=vm)
    dma = pltpu.SemaphoreType.DMA
    mine = pl.pallas_call(
        functools.partial(inbound_kernel, own, owners),
        out_shape=[wide] * 4,
        in_specs=[here] * 4,
        out_specs=[here] * 4,
        scratch_shapes=[dma((4,)), dma((4,)), dma((4,))],
        compiler_params=pltpu.CompilerParams(collective_id=0, has_side_effects=True),
    )(*[x.reshape(channels, steps) for x in (queries, key_stream, value_stream, cotangent)])
    rates = decay_rates.T
    size = jnp.sqrt(-jnp.expm1(-2.0 * rates))
    own_taps = lax.dynamic_slice(short_taps.reshape(3 * taps, channels), (0, me * own), (3 * taps, own))
    n_rows = 3 * modes + 3 * taps
    table = jnp.concatenate(
        [
            jnp.exp(-rates),
            rates,
            residues.T * size,
            own_taps,
            jnp.zeros((TABLE_EXTRA - n_rows, own), F32),
            size,
            residues.T,
        ]
    )
    line = steps * SUBS
    reach = taps - 1
    tap_rows = 16
    results = pl.pallas_call(
        functools.partial(owner_kernel, own, modes, taps, steps, scale),
        out_shape=[wide] * 4 + [jax.ShapeDtypeStruct((2 * modes + SUBS, LANES), F32)],
        in_specs=[pl.BlockSpec(memory_space=vm)] * 5,
        out_specs=[pl.BlockSpec(memory_space=vm)] * 5,
        scratch_shapes=[vm((line + reach * SUBS, LANES), F32)] * 4
        + [vm((line, LANES), F32)] * 7
        + [vm((line + reach * SUBS, LANES), F32)] * 3
        + [
            vm(((n_rows + modes) * SUBS, LANES), F32),
            vm((modes * SUBS, LANES), F32),
            vm((modes * SUBS, LANES), F32),
            vm((line * GROUP, LANES), F32),
            vm((modes, LANES), F32),
            vm((modes, LANES), F32),
            vm((tap_rows, LANES), F32),
        ],
        compiler_params=pltpu.CompilerParams(vmem_limit_bytes=48 * 1024 * 1024),
    )(*mine, table)
    used = -(-3 * taps * own // LANES)
    doubles = lax.axis_size("dp")
    small_shape = jax.ShapeDtypeStruct((2 * modes + SUBS, LANES), F32)
    *outs, small, shared = pl.pallas_call(
        functools.partial(outbound_kernel, own, owners, doubles, 2 * modes, used),
        out_shape=[wide] * 4 + [small_shape, jax.ShapeDtypeStruct((owners * SUBS, LANES), F32)],
        in_specs=[here] * 5,
        out_specs=[here] * 6,
        scratch_shapes=[
            vm((doubles,) + small_shape.shape, F32),
            dma((4,)),
            dma((4,)),
            dma((6,)),
            dma((doubles,)),
            dma((doubles,)),
            dma,
            dma,
        ],
        compiler_params=pltpu.CompilerParams(collective_id=1, has_side_effects=True),
    )(*results)
    outs = [x.reshape(queries.shape) for x in outs]
    tap_total = shared.reshape(owners, SUBS * LANES)[:, : 3 * taps * own].reshape(owners, 3, taps, own)
    tap_total = tap_total.transpose(1, 2, 0, 3).reshape(3, taps, channels)
    small = small[:, :own]
    return (*outs, tap_total, small[:modes].T, small[modes : 2 * modes].T)


def solution(mesh):
    stream = P("dp", None, "context")
    in_specs = (stream,) * 4 + (P(), P("context", None), P("context", None))
    out_specs = (stream,) * 4 + (P(), P("context", None), P("context", None))
    return jax.shard_map(per_device, mesh=mesh, in_specs=in_specs, out_specs=out_specs, check_vma=False)
```

```python
import functools
import math

import jax
import jax.numpy as jnp
from jax import lax
from jax.experimental import pallas as pl
from jax.experimental.pallas import tpu as pltpu
from jax.sharding import PartitionSpec as P

F32 = jnp.float32
BF16 = jnp.bfloat16
HIGHEST = lax.Precision.HIGHEST
LANES = 128
SUBS = 8
GROUP = 8


def rounded(x):
    return x.astype(BF16).astype(F32)


MESH = pl.DeviceIdType.MESH


def greet(axis, peers, me):
    barrier = pltpu.get_barrier_semaphore()

    def signal(step, carry):
        pl.semaphore_signal(barrier, inc=1, device_id={axis: lax.rem(me + step, peers)}, device_id_type=MESH)
        return carry

    lax.fori_loop(1, peers, signal, 0)
    return barrier


def exchange(own, peers, me, sources, targets, numbers, send_sem, recv_sem):
    def piece(i):
        return pl.ds(pl.multiple_of(i * own, own), own)

    def send(step, carry):
        peer = lax.rem(me + step, peers)
        for n, (source, target) in zip(numbers, zip(sources, targets)):
            pltpu.make_async_remote_copy(
                src_ref=source.at[piece(peer)],
                dst_ref=target.at[piece(me)],
                send_sem=send_sem.at[n],
                recv_sem=recv_sem.at[n],
                device_id={"context": peer},
                device_id_type=MESH,
            ).start()
        return carry

    lax.fori_loop(1, peers, send, 0)


def settle(rows, refs, numbers, sem):
    for n, ref in zip(numbers, refs):
        whole = ref.at[pl.ds(0, rows)]
        pltpu.make_async_copy(whole, whole, sem.at[n]).wait()


def keep(own, me, sources, targets, sem):
    spot = pl.ds(pl.multiple_of(me * own, own), own)
    copies = [
        pltpu.make_async_copy(source.at[spot], target.at[spot], sem.at[n])
        for n, (source, target) in enumerate(zip(sources, targets))
    ]
    for copy in copies:
        copy.start()
    return copies


def operator_kernel(
    own, modes, taps, steps, peers, doubles, used, scale,
    q_ref, k_ref, v_ref, c_ref, taps_ref, residue_ref, rate_ref,
    out_ref, dq_ref, dk_ref, dv_ref, total_ref, shared_ref,
    mq, mk, mv, mc, oo, oq, ok, ov,
    xq, xk, xv, xc, qs, ks, vs, gs, us, ys, ss, aq, ak, av,
    tab, lst, pst, adj, qacc, racc, tacc, small, slots,
    in_send, in_recv, out_send, out_recv, keep_sem, pair_send, pair_recv, tap_send, tap_recv,
):
    me = lax.axis_index("context")
    mine = lax.axis_index("dp")
    barrier = greet("context", peers, me)
    greet("dp", doubles, mine)
    sources, landed = (k_ref, v_ref, q_ref, c_ref), (mk, mv, mq, mc)
    results, outputs = (ok, ov, oo, oq), (dk_ref, dv_ref, out_ref, dq_ref)
    copies = keep(own, me, sources, landed, keep_sem)
    early, late = (0, 1), (2, 3)
    remote = own * (peers - 1)

    lane = lax.broadcasted_iota(jnp.int32, (SUBS, LANES), 1)
    sub = lax.broadcasted_iota(jnp.int32, (SUBS, LANES), 0)
    per_row = LANES // own
    chunk = sub * per_row + lane // own
    chunks = SUBS * per_row

    def later(x, by):
        if by < per_row:
            turned = pltpu.roll(x, own * by, 1)
            x = jnp.where(lane >= own * by, turned, pltpu.roll(turned, 1, 0))
        else:
            x = pltpu.roll(x, by // per_row, 0)
        return jnp.where(chunk >= by, x, 0.0)

    def earlier(x, by):
        if by < per_row:
            turned = pltpu.roll(x, LANES - own * by, 1)
            x = jnp.where(lane < LANES - own * by, turned, pltpu.roll(turned, SUBS - 1, 0))
        else:
            x = pltpu.roll(x, SUBS - by // per_row, 0)
        return jnp.where(chunk < chunks - by, x, 0.0)

    def at(t):
        return pl.ds(pl.multiple_of(t * SUBS, SUBS), SUBS)

    spread = (
        lax.broadcasted_iota(jnp.int32, (own, LANES), 0)
        == lax.broadcasted_iota(jnp.int32, (own, LANES), 1) % own
    ).astype(F32)
    turn = (((0,), (0,)), ((), ()))
    residue = lax.dot_general(residue_ref[...], spread, turn, precision=HIGHEST, preferred_element_type=F32)
    rate = lax.dot_general(rate_ref[...], spread, turn, precision=HIGHEST, preferred_element_type=F32)
    double = 2.0 * rate
    series = 1.0 - double / 7.0
    for n in range(6, 1, -1):
        series = 1.0 - double / float(n) * series
    size = jnp.sqrt(double * series)
    damp = jnp.exp(-rate)
    weighted = residue * size
    chosen = (
        lax.broadcasted_iota(jnp.int32, (LANES, LANES), 0)
        == lax.rem(me, per_row) * own + lax.broadcasted_iota(jnp.int32, (LANES, LANES), 1) % own
    ).astype(F32)
    block = pl.ds(pl.multiple_of(me // per_row * LANES, LANES), LANES)
    n_rows = 2 * modes + 3 * taps
    for m in range(modes):
        tab[pl.ds(m * SUBS, SUBS), :] = jnp.broadcast_to(damp[m : m + 1, :], (SUBS, LANES))
        tab[pl.ds((modes + m) * SUBS, SUBS), :] = jnp.broadcast_to(weighted[m : m + 1, :], (SUBS, LANES))
    far = jnp.exp(rate * (-float(steps)))
    for m in range(modes):
        tab[pl.ds((n_rows + m) * SUBS, SUBS), :] = jnp.broadcast_to(far[m : m + 1, :], (SUBS, LANES))
    for stream in range(3):
        picked = jnp.dot(taps_ref[stream, :, block], chosen, precision=HIGHEST, preferred_element_type=F32)
        for j in range(taps):
            tab[pl.ds((2 * modes + stream * taps + j) * SUBS, SUBS), :] = jnp.broadcast_to(
                picked[j : j + 1, :], (SUBS, LANES)
            )

    def entry(row):
        return tab[pl.ds(row * SUBS, SUBS), :]

    pl.semaphore_wait(barrier, peers + doubles - 2)
    exchange(own, peers, me, sources[:2], landed[:2], early, in_send, in_recv)
    exchange(own, peers, me, sources[2:], landed[2:], late, in_send, in_recv)

    ones = (
        lax.broadcasted_iota(jnp.int32, (LANES, LANES), 0)
        == lax.broadcasted_iota(jnp.int32, (LANES, LANES), 1)
    ).astype(BF16)

    def flipped(x):
        return lax.dot_general(ones, x, (((1,), (1,)), ((), ())), preferred_element_type=F32)

    reach = taps - 1
    head = reach * SUBS
    def unpack(src, dst):
        for i in range(SUBS):
            dst[pl.ds(head + i, steps, stride=SUBS), :] = flipped(src[pl.ds(i * LANES, LANES), :])

    def rim(x):
        for j in range(reach):
            x[pl.ds(j * SUBS, SUBS), :] = later(x[pl.ds(head + (steps - reach + j) * SUBS, SUBS), :], 1)

    def tap(stream, j):
        return entry(2 * modes + stream * taps + j)

    def filtered(x, stream, t):
        total = tap(stream, 0) * x[at(t + reach), :]
        for j in range(1, taps):
            total = total + tap(stream, j) * x[at(t + reach - j), :]
        return rounded(total)

    def pair_features(t, carry):
        key, value = filtered(xk, 1, t), filtered(xv, 2, t)
        ks[at(t), :] = key
        vs[at(t), :] = value
        gs[at(t), :] = rounded(key * value)
        return carry

    def query_features(t, carry):
        query = filtered(xq, 0, t)
        qs[at(t), :] = query
        us[at(t), :] = rounded(xc[at(t + reach), :] * query)
        return carry

    zero = jnp.zeros((SUBS, LANES), F32)
    zeros = tuple(zero for _ in range(modes))

    def ahead_step(t, carry):
        gated = gs[at(t), :]
        return tuple(entry(m) * carry[m] + gated for m in range(modes))

    def back_step(i, carry):
        upstream = us[at(steps - 1 - i), :]
        return tuple(entry(m) * carry[m] + upstream for m in range(modes))

    def chain_ahead(m, carry):
        power, total = tab[at(m + n_rows), :], lst[at(m), :]
        by = 1
        while by < chunks:
            total = total + power * later(total, by)
            power = power * power
            by *= 2
        lst[at(m), :] = later(total, 1)
        return carry

    def chain_back(m, carry):
        power, total = tab[at(m + n_rows), :], pst[at(m), :]
        by = 1
        while by < chunks:
            total = total + power * earlier(total, by)
            power = power * power
            by *= 2
        pst[at(m), :] = earlier(total, 1)
        return carry

    for copy in copies:
        copy.wait()
    settle(remote, landed[:2], early, in_recv)
    unpack(mk, xk)
    unpack(mv, xv)
    rim(xk)
    rim(xv)
    lax.fori_loop(0, steps, pair_features, 0, unroll=4)
    ends = lax.fori_loop(0, steps, ahead_step, zeros, unroll=4)
    for m in range(modes):
        lst[pl.ds(m * SUBS, SUBS), :] = ends[m]
    lax.fori_loop(0, modes, chain_ahead, 0)

    settle(remote, landed[2:], late, in_recv)
    unpack(mq, xq)
    unpack(mc, xc)
    rim(xq)
    lax.fori_loop(0, steps, query_features, 0, unroll=4)
    ends = lax.fori_loop(0, steps, back_step, zeros, unroll=4)
    for m in range(modes):
        pst[pl.ds(m * SUBS, SUBS), :] = ends[m]
    lax.fori_loop(0, modes, chain_back, 0)

    for group in range(0, modes, GROUP):
        members = range(group, group + GROUP)

        def backward(i, carry):
            t = steps - 1 - i
            upstream = us[at(t), :]
            total = zero if group == 0 else ss[at(t), :]
            new = []
            for n, m in enumerate(members):
                state = entry(m) * carry[n] + upstream
                adj[at(t * modes + m), :] = state
                total = total + entry(modes + m) * state
                new.append(state)
            ss[at(t), :] = total
            return tuple(new)

        lax.fori_loop(0, steps, backward, tuple(pst[pl.ds(m * SUBS, SUBS), :] for m in members), unroll=2)

    def closing(a):
        for j in range(reach):
            a[pl.ds((steps + j) * SUBS, SUBS), :] = earlier(a[pl.ds(j * SUBS, SUBS), :], 1)

    def gradient(a, stream, t):
        total = tap(stream, 0) * a[at(t), :]
        for j in range(1, taps):
            total = total + tap(stream, j) * a[at(t + j), :]
        return total

    def pack(src, dst):
        for i in range(SUBS):
            part = src[pl.ds(i, steps, stride=SUBS), :].astype(BF16)
            dst[pl.ds(i * LANES, LANES), :] = flipped(part).astype(BF16)

    def pair_products(t, carry):
        source = rounded(ss[at(t), :])
        new = []
        for n, (other, ref, x) in enumerate(((vs, ak, xk), (ks, av, xv))):
            grad = rounded(source * other[at(t), :])
            ref[at(t), :] = grad
            for j in range(taps):
                new.append(carry[n * taps + j] + grad * x[at(t + reach - j), :])
        return tuple(new)

    def pair_gradients(t, carry):
        ys[at(t), :] = gradient(ak, 1, t)
        ss[at(t), :] = gradient(av, 2, t)
        return carry

    tacc[...] = jnp.zeros(tacc.shape, F32)
    sums = lax.fori_loop(0, steps, pair_products, tuple(zero for _ in range(2 * taps)), unroll=2)
    closing(ak)
    closing(av)
    lax.fori_loop(0, steps, pair_gradients, 0, unroll=4)
    pack(ys, ok)
    pack(ss, ov)
    for n in range(2 * taps):
        tacc[pl.ds(taps + n, 1), :] = jnp.sum(sums[n], axis=0, keepdims=True)
    exchange(own, peers, me, results[:2], outputs[:2], early, out_send, out_recv)
    copies = keep(own, me, results[:2], outputs[:2], keep_sem)

    for group in range(0, modes, GROUP):
        members = range(group, group + GROUP)

        def forward(t, carry):
            states, firsts, seconds = carry
            gated = gs[at(t), :]
            upstream = us[at(t), :]
            total = zero if group == 0 else ys[at(t), :]
            new_s, new_f, new_r = [], [], []
            for n, m in enumerate(members):
                new_r.append(seconds[n] + states[n] * adj[at(t * modes + m), :])
                state = entry(m) * states[n] + gated
                new_f.append(firsts[n] + upstream * state)
                total = total + entry(modes + m) * state
                new_s.append(state)
            ys[at(t), :] = total
            return tuple(new_s), tuple(new_f), tuple(new_r)

        few = tuple(zero for _ in members)
        _, firsts, seconds = lax.fori_loop(
            0, steps, forward, (tuple(lst[pl.ds(m * SUBS, SUBS), :] for m in members), few, few), unroll=2
        )
        for n, m in enumerate(members):
            qacc[pl.ds(m, 1), :] = jnp.sum(firsts[n], axis=0, keepdims=True)
            racc[pl.ds(m, 1), :] = jnp.sum(seconds[n], axis=0, keepdims=True)

    def query_products(t, carry):
        mixed = rounded(ys[at(t), :])
        ys[at(t), :] = qs[at(t), :] * mixed
        grad = rounded(xc[at(t + reach), :] * mixed)
        aq[at(t), :] = grad
        return tuple(carry[j] + grad * xq[at(t + reach - j), :] for j in range(taps))

    def query_gradients(t, carry):
        ss[at(t), :] = gradient(aq, 0, t)
        return carry

    sums = lax.fori_loop(0, steps, query_products, tuple(zero for _ in range(taps)), unroll=2)
    for n in range(taps):
        tacc[pl.ds(n, 1), :] = jnp.sum(sums[n], axis=0, keepdims=True)

    def over_chunks(x):
        by = own
        while by < LANES:
            x = x + pltpu.roll(x, by, 1)
            by *= 2
        return x

    first = over_chunks(qacc[...])
    second = over_chunks(racc[...]) * damp
    small[pl.ds(0, modes), :] = scale * size * first
    bend = residue * (damp * damp / size) * first - weighted * second
    small[pl.ds(modes, modes), :] = scale * rate * bend
    total_taps = scale * over_chunks(tacc[...])
    part = lax.broadcasted_iota(jnp.int32, (1, LANES), 1) // own
    packed = jnp.zeros((SUBS, LANES), F32)
    for n in range(3 * taps):
        spot = (part == n % per_row) & (sub == n // per_row)
        packed = jnp.where(spot, total_taps[n : n + 1, :], packed)
    small[pl.ds(2 * modes, SUBS), :] = packed

    closing(aq)
    lax.fori_loop(0, steps, query_gradients, 0, unroll=4)
    pairs = [
        pltpu.make_async_remote_copy(
            src_ref=small,
            dst_ref=slots.at[mine],
            send_sem=pair_send.at[step],
            recv_sem=pair_recv.at[step],
            device_id={"dp": lax.rem(mine + step, doubles)},
            device_id_type=MESH,
        )
        for step in range(1, doubles)
    ]
    for pair in pairs:
        pair.start()
    own_small = pltpu.make_async_copy(small, slots.at[mine], keep_sem.at[4])
    own_small.start()
    pack(ys, oo)
    pack(ss, oq)
    own_small.wait()
    for pair in pairs:
        pair.wait()
    total = slots[0]
    for n in range(1, doubles):
        total = total + slots[n]
    total_ref[...] = total
    exchange(own, peers, me, results[2:], outputs[2:], late, out_send, out_recv)
    copies += [
        pltpu.make_async_copy(source.at[spot_of(own, me)], target.at[spot_of(own, me)], keep_sem.at[n])
        for n, source, target in zip(late, results[2:], outputs[2:])
    ]
    for copy in copies[2:]:
        copy.start()
    spot = pl.ds(pl.multiple_of(me * SUBS, SUBS), used)
    piece = total_ref.at[pl.ds(2 * modes, used)]

    def send(step, carry):
        pltpu.make_async_remote_copy(
            src_ref=piece,
            dst_ref=shared_ref.at[spot],
            send_sem=tap_send,
            recv_sem=tap_recv,
            device_id={"context": lax.rem(me + step, peers)},
            device_id_type=MESH,
        ).start()
        return carry

    lax.fori_loop(1, peers, send, 0)
    own_taps = pltpu.make_async_copy(piece, shared_ref.at[spot], keep_sem.at[5])
    own_taps.start()
    settle(remote, sources[:2], early, in_send)
    settle(remote, sources[2:], late, in_send)
    for copy in copies:
        copy.wait()
    own_taps.wait()
    for refs, sem in ((outputs, out_recv), (results, out_send)):
        settle(remote, refs, range(4), sem)
    whole = shared_ref.at[pl.ds(0, used * (peers - 1))]
    pltpu.make_async_copy(whole, whole, tap_recv).wait()
    pltpu.make_async_copy(whole, whole, tap_send).wait()


def spot_of(own, me):
    return pl.ds(pl.multiple_of(me * own, own), own)


def closing_kernel(own, modes, taps, *refs):
    sources, total_ref, shared_ref, targets = refs[:4], refs[4], refs[5], refs[6:10]
    taps_ref, residue_ref, rate_ref = refs[10:]
    for source, target in zip(sources, targets):
        target[0] = source[...]
    per_row = LANES // own
    part = lax.broadcasted_iota(jnp.int32, (per_row, LANES), 1) // own
    owner = lax.broadcasted_iota(jnp.int32, (per_row, LANES), 0)
    for b in range(taps_ref.shape[2] // LANES):
        for n in range(3 * taps):
            held = shared_ref[pl.ds(b * per_row * SUBS + n // per_row, per_row, stride=SUBS), :]
            held = jnp.where(part == n % per_row, held, 0.0)
            by = own
            while by < LANES:
                held = held + pltpu.roll(held, by, 1)
                by *= 2
            row = jnp.sum(jnp.where(part == owner, held, 0.0), axis=0, keepdims=True)
            taps_ref[n // taps, pl.ds(n % taps, 1), pl.ds(b * LANES, LANES)] = row
    pick = (
        lax.broadcasted_iota(jnp.int32, (own, LANES), 0) == lax.broadcasted_iota(jnp.int32, (own, LANES), 1)
    ).astype(F32)
    for ref, start in ((residue_ref, 0), (rate_ref, modes)):
        ref[...] = lax.dot_general(
            pick,
            total_ref[pl.ds(start, modes), :],
            (((1,), (1,)), ((), ())),
            precision=HIGHEST,
            preferred_element_type=F32,
        )


def per_device(queries, key_stream, value_stream, cotangent, short_taps, residues, decay_rates):
    channels, steps = queries.shape[1], queries.shape[2]
    own, modes = residues.shape
    taps = short_taps.shape[1]
    owners, doubles = lax.axis_size("context"), lax.axis_size("dp")
    scale = 1.0 / math.sqrt(queries.shape[0] * doubles * steps * owners)
    used = -(-3 * taps * own // LANES)
    wide = jax.ShapeDtypeStruct((channels, steps), BF16)
    small_shape = (2 * modes + SUBS, LANES)
    line, reach = steps * SUBS, taps - 1
    vm = pltpu.VMEM
    here = pl.BlockSpec(memory_space=vm)
    dma = pltpu.SemaphoreType.DMA
    n_rows = 2 * modes + 3 * taps
    tap_rows = -(-3 * taps // SUBS) * SUBS
    shared_shape = jax.ShapeDtypeStruct((owners * SUBS, LANES), F32)
    streams = [x.reshape(channels, steps) for x in (queries, key_stream, value_stream, cotangent)]
    results = pl.pallas_call(
        functools.partial(operator_kernel, own, modes, taps, steps, owners, doubles, used, scale),
        out_shape=[wide] * 4 + [jax.ShapeDtypeStruct(small_shape, F32), shared_shape],
        in_specs=[here] * 7,
        out_specs=[here] * 6,
        scratch_shapes=[vm((channels, steps), BF16)] * 8
        + [vm((line + reach * SUBS, LANES), F32)] * 4
        + [vm((line, LANES), F32)] * 7
        + [vm((line + reach * SUBS, LANES), F32)] * 3
        + [
            vm(((n_rows + modes) * SUBS, LANES), F32),
            vm((modes * SUBS, LANES), F32),
            vm((modes * SUBS, LANES), F32),
            vm((line * modes, LANES), F32),
            vm((modes, LANES), F32),
            vm((modes, LANES), F32),
            vm((tap_rows, LANES), F32),
            vm(small_shape, F32),
            vm((doubles,) + small_shape, F32),
        ]
        + [dma((4,))] * 4
        + [dma((6,)), dma((doubles,)), dma((doubles,)), dma, dma],
        compiler_params=pltpu.CompilerParams(collective_id=0, has_side_effects=True),
    )(*streams, short_taps, residues, decay_rates)
    mode_shape = jax.ShapeDtypeStruct(residues.shape, F32)
    return pl.pallas_call(
        functools.partial(closing_kernel, own, modes, taps),
        out_shape=[jax.ShapeDtypeStruct(queries.shape, BF16)] * 4
        + [jax.ShapeDtypeStruct(short_taps.shape, F32), mode_shape, mode_shape],
        in_specs=[here] * 6,
        out_specs=[here] * 7,
    )(*results)


def solution(mesh):
    stream = P("dp", None, "context")
    in_specs = (stream,) * 4 + (P(), P("context", None), P("context", None))
    out_specs = (stream,) * 4 + (P(), P("context", None), P("context", None))
    return jax.shard_map(per_device, mesh=mesh, in_specs=in_specs, out_specs=out_specs, check_vma=False)
```

```python
import functools
import math

import jax
import jax.numpy as jnp
from jax import lax
from jax.experimental import pallas as pl
from jax.experimental.pallas import tpu as pltpu
from jax.sharding import PartitionSpec as P

F32 = jnp.float32
BF16 = jnp.bfloat16
HIGHEST = lax.Precision.HIGHEST
LANES = 128
SUBS = 8
GROUP = 8
TALL = 8
WIDE = 4
PLANE = 8


def rounded(x):
    return x.astype(BF16).astype(F32)


MESH = pl.DeviceIdType.MESH


def place(index):
    return index // (TALL * WIDE), lax.rem(index // WIDE, TALL), lax.rem(index, WIDE)


def context_of(y, z, x):
    return (y * TALL + z) * WIDE + x


def settle(ref, send, recv=None):
    pltpu.make_async_copy(ref, ref, send).wait()
    if recv is not None:
        pltpu.make_async_copy(ref, ref, recv).wait()


def operator_kernel(
    modes, taps, steps, doubles, scale,
    q_ref, k_ref, v_ref, c_ref, taps_ref, residue_ref, rate_ref,
    out_ref, dq_ref, dk_ref, dv_ref, shared_ref, dres_ref, drate_ref,
    mq, mk, mv, mc, oo, oq, ok, ov,
    xq, xk, xv, xc, qs, ks, vs, gs, us, ys, ss, aq, ak, av,
    tab, logs, lst, pst, past, qacc, racc, tacc,
    tsrc, tin, fsrc, fin, bsrc, bin_, rims, tails, small, stack, slots, total_ref,
    in_send, in_recv, out_send, out_recv, keep_sem, pair_send, pair_recv,
    rim_send, rim_recv, tail_send, tail_recv, line_send, line_recv, tap_send, tap_recv,
):
    y, z, x = place(lax.axis_index("context"))
    mine = lax.axis_index("dp")
    spot = y * WIDE + x
    own = residue_ref.shape[0]
    barrier = pltpu.get_barrier_semaphore()

    def across(step):
        s = lax.rem(spot + step, PLANE)
        return s, {"context": context_of(s // WIDE, z, lax.rem(s, WIDE))}

    def along(step):
        return {"context": context_of(y, lax.rem(z + step, TALL), x)}

    for step in range(1, PLANE):
        pl.semaphore_signal(barrier, inc=1, device_id=across(step)[1], device_id_type=MESH)
    for step in range(1, TALL):
        pl.semaphore_signal(barrier, inc=1, device_id=along(step), device_id_type=MESH)
    for step in range(1, doubles):
        pl.semaphore_signal(
            barrier, inc=1, device_id={"dp": lax.rem(mine + step, doubles)}, device_id_type=MESH
        )

    sources, landed = (k_ref, v_ref, q_ref, c_ref), (mk, mv, mq, mc)
    kept = [
        pltpu.make_async_copy(sources[n].at[y, :, x], landed[n].at[spot], keep_sem.at[n]) for n in range(4)
    ]
    for copy in kept:
        copy.start()

    lane = lax.broadcasted_iota(jnp.int32, (SUBS, LANES), 1)
    sub = lax.broadcasted_iota(jnp.int32, (SUBS, LANES), 0)
    step_x = lax.rem(sub, WIDE)
    high = sub >= WIDE

    def at(t):
        return pl.ds(pl.multiple_of(t * SUBS, SUBS), SUBS)

    def fixed(row):
        return pl.ds(row * SUBS, SUBS)

    mine_lanes = (
        lax.broadcasted_iota(jnp.int32, (own, LANES), 1)
        == z * own + lax.broadcasted_iota(jnp.int32, (own, LANES), 0)
    ).astype(F32)
    turn = (((0,), (0,)), ((), ()))
    tsrc[pl.ds(0, modes), :] = lax.dot_general(
        residue_ref[...], mine_lanes, turn, precision=HIGHEST, preferred_element_type=F32
    )
    tsrc[pl.ds(modes, modes), :] = lax.dot_general(
        rate_ref[...], mine_lanes, turn, precision=HIGHEST, preferred_element_type=F32
    )
    half = taps_ref.shape[2] // 2
    column = lax.broadcasted_iota(jnp.int32, (half, LANES), 1)
    chosen = (
        lax.broadcasted_iota(jnp.int32, (half, LANES), 0)
        == column // own * (WIDE * own) + x * own + lax.rem(column, own)
    ).astype(F32)
    block = pl.ds(pl.multiple_of(y * half, half), half)
    n_taps = 2 * modes
    for stream in range(3):
        picked = jnp.dot(taps_ref[stream, :, block], chosen, precision=HIGHEST, preferred_element_type=F32)
        for j in range(taps):
            tab[fixed(n_taps + stream * taps + j), :] = jnp.broadcast_to(picked[j : j + 1, :], (SUBS, LANES))
    tacc[...] = jnp.zeros(tacc.shape, F32)

    def line(src, dst, n):
        for step in range(1, TALL):
            pltpu.make_async_remote_copy(
                src_ref=src,
                dst_ref=dst.at[z],
                send_sem=line_send.at[n],
                recv_sem=line_recv.at[n],
                device_id=along(step),
                device_id_type=MESH,
            ).start()
        copy = pltpu.make_async_copy(src, dst.at[z], keep_sem.at[8 + n])
        copy.start()
        return copy

    def line_wait(copy, dst, n):
        copy.wait()
        settle(dst.at[pl.ds(0, TALL - 1)], line_send.at[n], line_recv.at[n])

    pl.semaphore_wait(barrier, PLANE + TALL + doubles - 3)
    table_copy = line(tsrc, tin, 0)
    for n in range(4):
        for step in range(1, PLANE):
            s, peer = across(step)
            pltpu.make_async_remote_copy(
                src_ref=sources[n].at[s // WIDE, :, lax.rem(s, WIDE)],
                dst_ref=landed[n].at[spot],
                send_sem=in_send.at[n],
                recv_sem=in_recv.at[n],
                device_id=peer,
                device_id_type=MESH,
            ).start()

    line_wait(table_copy, tin, 0)
    tables = tin[0]
    for n in range(1, TALL):
        tables = tables + tin[n]
    residue, rate = tables[:modes], tables[modes:]
    double = 2.0 * rate
    series = 1.0 - double / 7.0
    for n in range(6, 1, -1):
        series = 1.0 - double / float(n) * series
    size = jnp.sqrt(double * series)
    damp = jnp.exp(-rate)
    weighted = residue * size
    for m in range(modes):
        tab[fixed(m), :] = jnp.broadcast_to(damp[m : m + 1, :], (SUBS, LANES))
        tab[fixed(modes + m), :] = jnp.broadcast_to(weighted[m : m + 1, :], (SUBS, LANES))
        logs[fixed(m), :] = jnp.broadcast_to(-float(steps) * rate[m : m + 1, :], (SUBS, LANES))

    def entry(row):
        return tab[fixed(row), :]

    ones = (
        lax.broadcasted_iota(jnp.int32, (LANES, LANES), 0)
        == lax.broadcasted_iota(jnp.int32, (LANES, LANES), 1)
    ).astype(BF16)

    def flipped(value):
        return lax.dot_general(ones, value, (((1,), (1,)), ((), ())), preferred_element_type=F32)

    reach = taps - 1
    head = reach * SUBS

    def unpack(n, dst):
        kept[n].wait()
        settle(landed[n].at[pl.ds(0, PLANE - 1)], in_recv.at[n])
        for i in range(PLANE):
            dst[pl.ds(head + i, steps, stride=SUBS), :] = flipped(landed[n][i].reshape(LANES, steps))

    def rim_copy(n, src):
        return pltpu.make_async_remote_copy(
            src_ref=src.at[pl.ds(steps * SUBS, head)],
            dst_ref=rims.at[n],
            send_sem=rim_send.at[n],
            recv_sem=rim_recv.at[n],
            device_id=along(1),
            device_id_type=MESH,
        )

    def tail_copy(n, src):
        return pltpu.make_async_remote_copy(
            src_ref=src.at[pl.ds(0, head)],
            dst_ref=tails.at[n],
            send_sem=tail_send.at[n],
            recv_sem=tail_recv.at[n],
            device_id=along(TALL - 1),
            device_id_type=MESH,
        )

    first_z, last_z = z == 0, z == TALL - 1

    def before(value, outer):
        lowest = jnp.where(high, pltpu.roll(outer, 1, 0), 0.0)
        outer = jnp.where(first_z, lowest, pltpu.roll(outer, 5, 0))
        return jnp.where(step_x > 0, pltpu.roll(value, 1, 0), outer)

    def after(value, outer):
        highest = jnp.where(high, 0.0, pltpu.roll(outer, 7, 0))
        outer = jnp.where(last_z, highest, pltpu.roll(outer, 3, 0))
        return jnp.where(step_x < WIDE - 1, pltpu.roll(value, 7, 0), outer)

    def rim(n, ref):
        for j in range(reach):
            ref[fixed(j), :] = before(ref[fixed(steps + j), :], rims[n, fixed(j), :])

    def tail(n, ref):
        for j in range(reach):
            ref[fixed(steps + j), :] = after(ref[fixed(j), :], tails[n, fixed(j), :])

    def tap(stream, j):
        return entry(n_taps + stream * taps + j)

    def filtered(ref, stream, t):
        total = tap(stream, 0) * ref[at(t + reach), :]
        for j in range(1, taps):
            total = total + tap(stream, j) * ref[at(t + reach - j), :]
        return rounded(total)

    def pair_features(t, carry):
        key, value = filtered(xk, 1, t), filtered(xv, 2, t)
        ks[at(t), :] = key
        vs[at(t), :] = value
        gs[at(t), :] = rounded(key * value)
        return carry

    def query_features(t, carry):
        query = filtered(xq, 0, t)
        qs[at(t), :] = query
        us[at(t), :] = rounded(xc[at(t + reach), :] * query)
        return carry

    zero = jnp.zeros((SUBS, LANES), F32)
    zeros = tuple(zero for _ in range(modes))

    def ahead_step(t, carry):
        gated = gs[at(t), :]
        return tuple(entry(m) * carry[m] + gated for m in range(modes))

    def back_step(i, carry):
        upstream = us[at(steps - 1 - i), :]
        return tuple(entry(m) * carry[m] + upstream for m in range(modes))

    def scan_ahead(value, m):
        power = jnp.exp(logs[fixed(m), :])
        for by in (1, 2):
            value = value + power * jnp.where(step_x >= by, pltpu.roll(value, by, 0), 0.0)
            power = power * power
        return value

    def scan_back(value, m):
        power = jnp.exp(logs[fixed(m), :])
        for by in (1, 2):
            value = value + power * jnp.where(step_x < WIDE - by, pltpu.roll(value, SUBS - by, 0), 0.0)
            power = power * power
        return value

    def ahead_row(n):
        return step_x == WIDE - 1 - n

    def back_row(n):
        return step_x == n

    def finish_ends(ends, scan, store, src, row_of, sign):
        for g in range(modes // WIDE):
            packed = zero
            for n in range(WIDE):
                m = g * WIDE + n
                value = scan(ends[m], m)
                store[fixed(m), :] = value
                packed = jnp.where(row_of(n), value if n == 0 else pltpu.roll(value, (sign * n) % SUBS, 0), packed)
            src[fixed(g), :] = packed

    def seeds(store, held, row_of, sign, order, inside, leap, fresh, weight):
        for g in range(modes // WIDE):
            slow = zero
            for n in range(WIDE):
                slow = jnp.where(row_of(n), logs[fixed(g * WIDE + n), :], slow)
            far = jnp.exp(float(WIDE) * slow)
            full, part = zero, zero
            for other in order:
                value = held[other, fixed(g), :]
                full = far * full + value
                part = jnp.where(inside(other), far * part + value, part)
            part = part + jnp.where(fresh, jnp.exp(slow * leap) * pltpu.roll(full, WIDE, 0), 0.0)
            for n in range(WIDE):
                m = g * WIDE + n
                value = jnp.where(row_of(n), part, 0.0)
                if n:
                    value = pltpu.roll(value, (-sign * n) % SUBS, 0)
                value = value + pltpu.roll(value, sign % SUBS, 0)
                value = value + pltpu.roll(value, (2 * sign) % SUBS, 0)
                value = jnp.exp(logs[fixed(m), :] * weight) * value
                near = pltpu.roll(store[fixed(m), :], (-sign) % SUBS, 0)
                keep = step_x > 0 if sign < 0 else step_x < WIDE - 1
                store[fixed(m), :] = jnp.where(keep, near, 0.0) + value

    float_x = step_x.astype(F32)
    float_z = z.astype(F32)

    unpack(0, xk)
    unpack(1, xv)
    rim_copies = [rim_copy(0, xk), rim_copy(1, xv)]
    for copy in rim_copies:
        copy.start()
    unpack(2, xq)
    for copy in rim_copies:
        copy.wait()
    rim(0, xk)
    rim(1, xv)
    rim_copies = [rim_copy(2, xq)]
    rim_copies[0].start()
    lax.fori_loop(0, steps, pair_features, 0, unroll=4)
    ends = lax.fori_loop(0, steps, ahead_step, zeros, unroll=4)
    finish_ends(ends, scan_ahead, lst, fsrc, ahead_row, -1)
    rim_copies[0].wait()
    rim(2, xq)
    ahead_copy = line(fsrc, fin, 1)

    unpack(3, xc)
    lax.fori_loop(0, steps, query_features, 0, unroll=4)
    ends = lax.fori_loop(0, steps, back_step, zeros, unroll=4)
    finish_ends(ends, scan_back, pst, bsrc, back_row, 1)
    line_wait(ahead_copy, fin, 1)
    back_copy = line(bsrc, bin_, 2)
    seeds(
        lst, fin, ahead_row, -1, range(TALL), lambda other: other < z, float(WIDE) * float_z, high, float_x
    )

    for group in range(0, modes, GROUP):
        members = range(group, group + GROUP)

        def forward(t, carry):
            states, firsts = carry
            gated = gs[at(t), :]
            upstream = us[at(t), :]
            total = zero if group == 0 else ys[at(t), :]
            new_s, new_f = [], []
            for n, m in enumerate(members):
                past[at(t * modes + m), :] = states[n]
                state = entry(m) * states[n] + gated
                new_f.append(firsts[n] + upstream * state)
                total = total + entry(modes + m) * state
                new_s.append(state)
            ys[at(t), :] = total
            return tuple(new_s), tuple(new_f)

        few = tuple(zero for _ in members)
        _, firsts = lax.fori_loop(0, steps, forward, (tuple(lst[fixed(m), :] for m in members), few), unroll=2)
        for n, m in enumerate(members):
            qacc[pl.ds(m, 1), :] = jnp.sum(firsts[n], axis=0, keepdims=True)

    def gradient(a, stream, t):
        total = tap(stream, 0) * a[at(t), :]
        for j in range(1, taps):
            total = total + tap(stream, j) * a[at(t + j), :]
        return total

    def pack(src, dst):
        for i in range(PLANE):
            value = src[pl.ds(i, steps, stride=SUBS), :].astype(BF16)
            dst[i] = flipped(value).astype(BF16).reshape(dst.shape[1:])

    def query_products(t, carry):
        mixed = rounded(ys[at(t), :])
        ys[at(t), :] = qs[at(t), :] * mixed
        grad = rounded(xc[at(t + reach), :] * mixed)
        aq[at(t), :] = grad
        return tuple(carry[j] + grad * xq[at(t + reach - j), :] for j in range(taps))

    def query_gradients(t, carry):
        ss[at(t), :] = gradient(aq, 0, t)
        return carry

    results, outputs = (oo, oq, ok, ov), (out_ref, dq_ref, dk_ref, dv_ref)
    kept_out = []

    def deliver(n):
        for step in range(1, PLANE):
            s, peer = across(step)
            pltpu.make_async_remote_copy(
                src_ref=results[n].at[s],
                dst_ref=outputs[n].at[y, :, x],
                send_sem=out_send.at[n],
                recv_sem=out_recv.at[n],
                device_id=peer,
                device_id_type=MESH,
            ).start()
        copy = pltpu.make_async_copy(results[n].at[spot], outputs[n].at[y, :, x], keep_sem.at[4 + n])
        copy.start()
        kept_out.append(copy)

    sums = lax.fori_loop(0, steps, query_products, tuple(zero for _ in range(taps)), unroll=2)
    for n in range(taps):
        tacc[pl.ds(n, 1), :] = jnp.sum(sums[n], axis=0, keepdims=True)
    query_tail = tail_copy(0, aq)
    query_tail.start()
    pack(ys, oo)
    line_wait(back_copy, bin_, 2)
    deliver(0)
    seeds(
        pst, bin_, back_row, 1, range(TALL - 1, -1, -1), lambda other: other > z,
        float(WIDE) * (float(TALL - 1) - float_z), jnp.logical_not(high), float(WIDE - 1) - float_x,
    )
    query_tail.wait()
    tail(0, aq)
    lax.fori_loop(0, steps, query_gradients, 0, unroll=4)
    pack(ss, oq)

    for group in range(0, modes, GROUP):
        members = range(group, group + GROUP)

        def backward(i, carry):
            states, seconds = carry
            t = steps - 1 - i
            upstream = us[at(t), :]
            total = zero if group == 0 else ss[at(t), :]
            new_s, new_r = [], []
            for n, m in enumerate(members):
                state = entry(m) * states[n] + upstream
                new_r.append(seconds[n] + state * past[at(t * modes + m), :])
                total = total + entry(modes + m) * state
                new_s.append(state)
            ss[at(t), :] = total
            return tuple(new_s), tuple(new_r)

        few = tuple(zero for _ in members)
        _, seconds = lax.fori_loop(0, steps, backward, (tuple(pst[fixed(m), :] for m in members), few), unroll=2)
        for n, m in enumerate(members):
            racc[pl.ds(m, 1), :] = jnp.sum(seconds[n], axis=0, keepdims=True)
        if group == 0:
            deliver(1)

    def pair_products(t, carry):
        source = rounded(ss[at(t), :])
        new = []
        for n, (other, ref, x_ref) in enumerate(((vs, ak, xk), (ks, av, xv))):
            grad = rounded(source * other[at(t), :])
            ref[at(t), :] = grad
            for j in range(taps):
                new.append(carry[n * taps + j] + grad * x_ref[at(t + reach - j), :])
        return tuple(new)

    def pair_gradients(t, carry):
        ys[at(t), :] = gradient(ak, 1, t)
        ss[at(t), :] = gradient(av, 2, t)
        return carry

    sums = lax.fori_loop(0, steps, pair_products, tuple(zero for _ in range(2 * taps)), unroll=2)
    for n in range(2 * taps):
        tacc[pl.ds(taps + n, 1), :] = jnp.sum(sums[n], axis=0, keepdims=True)
    tail_copies = [tail_copy(1, ak), tail_copy(2, av)]
    for copy in tail_copies:
        copy.start()
    first, second = qacc[...], racc[...] * damp
    small[pl.ds(0, modes), :] = scale * size * first
    small[pl.ds(modes, modes), :] = scale * rate * (residue * (damp * damp / size) * first - weighted * second)
    small[pl.ds(2 * modes, tacc.shape[0]), :] = scale * tacc[...]
    for copy in tail_copies:
        copy.wait()
    small_copy = line(small, stack, 3)
    tail(1, ak)
    tail(2, av)
    lax.fori_loop(0, steps, pair_gradients, 0, unroll=4)
    pack(ys, ok)
    pack(ss, ov)

    line_wait(small_copy, stack, 3)
    total = stack[0]
    for n in range(1, TALL):
        total = total + stack[n]
    slots[doubles] = total
    deliver(2)
    deliver(3)
    pairs = [
        pltpu.make_async_remote_copy(
            src_ref=slots.at[doubles],
            dst_ref=slots.at[mine],
            send_sem=pair_send.at[step],
            recv_sem=pair_recv.at[step],
            device_id={"dp": lax.rem(mine + step, doubles)},
            device_id_type=MESH,
        )
        for step in range(1, doubles)
    ]
    for pair in pairs:
        pair.start()
    own_small = pltpu.make_async_copy(slots.at[doubles], slots.at[mine], keep_sem.at[12])
    own_small.start()
    own_small.wait()
    for pair in pairs:
        pair.wait()
    total = slots[0]
    for n in range(1, doubles):
        total = total + slots[n]
    total_ref[...] = total[2 * modes :]
    for ref, start in ((dres_ref, 0), (drate_ref, modes)):
        ref[...] = lax.dot_general(
            mine_lanes,
            total[start : start + modes],
            (((1,), (1,)), ((), ())),
            precision=HIGHEST,
            preferred_element_type=F32,
        )
    for step in range(1, PLANE):
        pltpu.make_async_remote_copy(
            src_ref=total_ref,
            dst_ref=shared_ref.at[spot],
            send_sem=tap_send,
            recv_sem=tap_recv,
            device_id=across(step)[1],
            device_id_type=MESH,
        ).start()
    own_taps = pltpu.make_async_copy(total_ref, shared_ref.at[spot], keep_sem.at[13])
    own_taps.start()
    for n in range(4):
        settle(landed[n].at[pl.ds(0, PLANE - 1)], in_send.at[n])
    for copy in kept_out:
        copy.wait()
    own_taps.wait()
    for n in range(4):
        settle(results[n].at[pl.ds(0, PLANE - 1)], out_send.at[n])
        settle(outputs[n].at[:, pl.ds(0, TALL - 1)], out_recv.at[n])
    settle(shared_ref.at[pl.ds(0, PLANE - 1)], tap_send, tap_recv)


def closing_kernel(own, taps, *refs):
    sources, shared_ref, parts, targets = refs[:4], refs[4], refs[5:7], refs[7:11]
    taps_ref, finals = refs[11], refs[12:]
    for source, target in zip(sources, targets):
        target[0] = source[...].reshape(target.shape[1:])
    for part, final in zip(parts, finals):
        final[...] = part[...]
    rows = shared_ref.shape[1]
    group = lax.broadcasted_iota(jnp.int32, (rows, LANES), 1) // own
    groups = LANES // own
    for b in range(taps_ref.shape[2] // LANES):
        y, pair = b // WIDE, b % WIDE
        value = jnp.zeros((rows, LANES), F32)
        for spot in range(groups):
            z, x = pair * (groups // WIDE) + spot // WIDE, spot % WIDE
            held = shared_ref[y * WIDE + x]
            held = pltpu.roll(held, (spot - z) * own % LANES, 1)
            value = jnp.where(group == spot, held, value)
        for stream in range(3):
            taps_ref[stream, :, pl.ds(b * LANES, LANES)] = value[stream * taps : (stream + 1) * taps]


def per_device(queries, key_stream, value_stream, cotangent, short_taps, residues, decay_rates):
    channels, steps = queries.shape[1], queries.shape[2]
    own, modes = residues.shape
    taps = short_taps.shape[1]
    owners, doubles = lax.axis_size("context"), lax.axis_size("dp")
    scale = 1.0 / math.sqrt(queries.shape[0] * doubles * steps * owners)
    view = (owners // (TALL * WIDE), TALL, WIDE, own, steps)
    wide = jax.ShapeDtypeStruct(view, BF16)
    mode_shape = jax.ShapeDtypeStruct(residues.shape, F32)
    line, reach = steps * SUBS, taps - 1
    vm = pltpu.VMEM
    here = pl.BlockSpec(memory_space=vm)
    dma = pltpu.SemaphoreType.DMA
    tap_rows = -(-3 * taps // SUBS) * SUBS
    rows = 2 * modes + tap_rows
    ends = modes // WIDE * SUBS
    streams = [x.reshape(view) for x in (queries, key_stream, value_stream, cotangent)]
    results = pl.pallas_call(
        functools.partial(operator_kernel, modes, taps, steps, doubles, scale),
        out_shape=[wide] * 4 + [jax.ShapeDtypeStruct((PLANE, tap_rows, LANES), F32), mode_shape, mode_shape],
        in_specs=[here] * 7,
        out_specs=[here] * 7,
        scratch_shapes=[vm((PLANE, TALL, own, steps), BF16)] * 8
        + [vm((line + reach * SUBS, LANES), F32)] * 4
        + [vm((line, LANES), F32)] * 7
        + [vm((line + reach * SUBS, LANES), F32)] * 3
        + [
            vm(((2 * modes + 3 * taps) * SUBS, LANES), F32),
            vm((modes * SUBS, LANES), F32),
            vm((modes * SUBS, LANES), F32),
            vm((modes * SUBS, LANES), F32),
            vm((line * modes, LANES), F32),
            vm((modes, LANES), F32),
            vm((modes, LANES), F32),
            vm((tap_rows, LANES), F32),
            vm((2 * modes, LANES), F32),
            vm((TALL, 2 * modes, LANES), F32),
            vm((ends, LANES), F32),
            vm((TALL, ends, LANES), F32),
            vm((ends, LANES), F32),
            vm((TALL, ends, LANES), F32),
            vm((3, reach * SUBS, LANES), F32),
            vm((3, reach * SUBS, LANES), F32),
            vm((rows, LANES), F32),
            vm((TALL, rows, LANES), F32),
            vm((doubles + 1, rows, LANES), F32),
            vm((tap_rows, LANES), F32),
        ]
        + [dma((4,))] * 4
        + [dma((14,)), dma((doubles,)), dma((doubles,))]
        + [dma((3,))] * 4
        + [dma((4,))] * 2
        + [dma, dma],
        compiler_params=pltpu.CompilerParams(collective_id=0, has_side_effects=True),
    )(*streams, short_taps, residues, decay_rates)
    return pl.pallas_call(
        functools.partial(closing_kernel, own, taps),
        out_shape=[jax.ShapeDtypeStruct(queries.shape, BF16)] * 4
        + [jax.ShapeDtypeStruct(short_taps.shape, F32), mode_shape, mode_shape],
        in_specs=[here] * 7,
        out_specs=[here] * 7,
    )(*results)


def solution(mesh):
    stream = P("dp", None, "context")
    in_specs = (stream,) * 4 + (P(), P("context", None), P("context", None))
    out_specs = (stream,) * 4 + (P(), P("context", None), P("context", None))
    return jax.shard_map(per_device, mesh=mesh, in_specs=in_specs, out_specs=out_specs, check_vma=False)
```

```python
import functools
import math

import jax
import jax.numpy as jnp
from jax import lax
from jax.experimental import pallas as pl
from jax.experimental.pallas import tpu as pltpu
from jax.sharding import PartitionSpec as P

F32 = jnp.float32
BF16 = jnp.bfloat16
HIGHEST = lax.Precision.HIGHEST
LANES = 128
SUBS = 8
GROUP = 8
TALL = 8
WIDE = 4
PLANE = 8


def rounded(x):
    return x.astype(BF16).astype(F32)


MESH = pl.DeviceIdType.MESH


def place(index):
    return index // (TALL * WIDE), lax.rem(index // WIDE, TALL), lax.rem(index, WIDE)


def context_of(y, z, x):
    return (y * TALL + z) * WIDE + x


def settle(ref, send, recv=None):
    pltpu.make_async_copy(ref, ref, send).wait()
    if recv is not None:
        pltpu.make_async_copy(ref, ref, recv).wait()


def operator_kernel(
    modes, taps, steps, doubles, scale,
    q_ref, k_ref, v_ref, c_ref, taps_ref, residue_ref, rate_ref,
    out_ref, dq_ref, dk_ref, dv_ref, shared_ref, dres_ref, drate_ref,
    mq, mk, mv, mc, oo, oq, ok, ov,
    xq, xk, xv, xc, qs, ks, vs, gs, us, ys, ss, aq, ak, av,
    tab, logs, lst, pst, past, qacc, racc, tacc,
    tsrc, tin, fsrc, fin, bsrc, bin_, rims, tails,
    tap_part, tap_stack, tap_slots, mode_part, mode_stack, mode_slots, total_ref,
    in_send, in_recv, out_send, out_recv, keep_sem, pair_send, pair_recv,
    rim_send, rim_recv, tail_send, tail_recv, line_send, line_recv, tap_send, tap_recv,
):
    y, z, x = place(lax.axis_index("context"))
    mine = lax.axis_index("dp")
    spot = y * WIDE + x
    own = residue_ref.shape[0]
    barrier = pltpu.get_barrier_semaphore()

    def across(step):
        s = lax.rem(spot + step, PLANE)
        return s, {"context": context_of(s // WIDE, z, lax.rem(s, WIDE))}

    def along(step):
        return {"context": context_of(y, lax.rem(z + step, TALL), x)}

    for step in range(1, PLANE):
        pl.semaphore_signal(barrier, inc=1, device_id=across(step)[1], device_id_type=MESH)
    for step in range(1, TALL):
        pl.semaphore_signal(barrier, inc=1, device_id=along(step), device_id_type=MESH)
    for step in range(1, doubles):
        pl.semaphore_signal(
            barrier, inc=1, device_id={"dp": lax.rem(mine + step, doubles)}, device_id_type=MESH
        )

    sources, landed = (k_ref, v_ref, q_ref, c_ref), (mk, mv, mq, mc)
    kept = [
        pltpu.make_async_copy(sources[n].at[y, :, x], landed[n].at[spot], keep_sem.at[n]) for n in range(4)
    ]
    for copy in kept:
        copy.start()

    lane = lax.broadcasted_iota(jnp.int32, (SUBS, LANES), 1)
    sub = lax.broadcasted_iota(jnp.int32, (SUBS, LANES), 0)
    step_x = lax.rem(sub, WIDE)
    high = sub >= WIDE

    def at(t):
        return pl.ds(pl.multiple_of(t * SUBS, SUBS), SUBS)

    def fixed(row):
        return pl.ds(row * SUBS, SUBS)

    mine_lanes = (
        lax.broadcasted_iota(jnp.int32, (own, LANES), 1)
        == z * own + lax.broadcasted_iota(jnp.int32, (own, LANES), 0)
    ).astype(F32)
    turn = (((0,), (0,)), ((), ()))
    tsrc[pl.ds(0, modes), :] = lax.dot_general(
        residue_ref[...], mine_lanes, turn, precision=HIGHEST, preferred_element_type=F32
    )
    tsrc[pl.ds(modes, modes), :] = lax.dot_general(
        rate_ref[...], mine_lanes, turn, precision=HIGHEST, preferred_element_type=F32
    )
    half = taps_ref.shape[2] // 2
    column = lax.broadcasted_iota(jnp.int32, (half, LANES), 1)
    chosen = (
        lax.broadcasted_iota(jnp.int32, (half, LANES), 0)
        == column // own * (WIDE * own) + x * own + lax.rem(column, own)
    ).astype(F32)
    block = pl.ds(pl.multiple_of(y * half, half), half)
    n_taps = 2 * modes
    for stream in range(3):
        picked = jnp.dot(taps_ref[stream, :, block], chosen, precision=HIGHEST, preferred_element_type=F32)
        for j in range(taps):
            tab[fixed(n_taps + stream * taps + j), :] = jnp.broadcast_to(picked[j : j + 1, :], (SUBS, LANES))
    tacc[...] = jnp.zeros(tacc.shape, F32)

    def line(src, dst, n):
        for step in range(1, TALL):
            pltpu.make_async_remote_copy(
                src_ref=src,
                dst_ref=dst.at[z],
                send_sem=line_send.at[n],
                recv_sem=line_recv.at[n],
                device_id=along(step),
                device_id_type=MESH,
            ).start()
        copy = pltpu.make_async_copy(src, dst.at[z], keep_sem.at[8 + n])
        copy.start()
        return copy

    def line_wait(copy, dst, n):
        copy.wait()
        settle(dst.at[pl.ds(0, TALL - 1)], line_send.at[n], line_recv.at[n])

    pl.semaphore_wait(barrier, PLANE + TALL + doubles - 3)
    table_copy = line(tsrc, tin, 0)
    for n in range(4):
        for step in range(1, PLANE):
            s, peer = across(step)
            pltpu.make_async_remote_copy(
                src_ref=sources[n].at[s // WIDE, :, lax.rem(s, WIDE)],
                dst_ref=landed[n].at[spot],
                send_sem=in_send.at[n],
                recv_sem=in_recv.at[n],
                device_id=peer,
                device_id_type=MESH,
            ).start()

    line_wait(table_copy, tin, 0)
    tables = tin[0]
    for n in range(1, TALL):
        tables = tables + tin[n]
    residue, rate = tables[:modes], tables[modes:]
    double = 2.0 * rate
    series = 1.0 - double / 7.0
    for n in range(6, 1, -1):
        series = 1.0 - double / float(n) * series
    size = jnp.sqrt(double * series)
    damp = jnp.exp(-rate)
    weighted = residue * size
    for m in range(modes):
        tab[fixed(m), :] = jnp.broadcast_to(damp[m : m + 1, :], (SUBS, LANES))
        tab[fixed(modes + m), :] = jnp.broadcast_to(weighted[m : m + 1, :], (SUBS, LANES))
        logs[fixed(m), :] = jnp.broadcast_to(-float(steps) * rate[m : m + 1, :], (SUBS, LANES))

    def entry(row):
        return tab[fixed(row), :]

    ones = (
        lax.broadcasted_iota(jnp.int32, (LANES, LANES), 0)
        == lax.broadcasted_iota(jnp.int32, (LANES, LANES), 1)
    ).astype(BF16)

    def flipped(value):
        return lax.dot_general(ones, value, (((1,), (1,)), ((), ())), preferred_element_type=F32)

    reach = taps - 1
    head = reach * SUBS

    def unpack(n, dst):
        kept[n].wait()
        settle(landed[n].at[pl.ds(0, PLANE - 1)], in_recv.at[n])
        for i in range(PLANE):
            dst[pl.ds(head + i, steps, stride=SUBS), :] = flipped(landed[n][i].reshape(LANES, steps))

    def rim_copy(n, src):
        return pltpu.make_async_remote_copy(
            src_ref=src.at[pl.ds(steps * SUBS, head)],
            dst_ref=rims.at[n],
            send_sem=rim_send.at[n],
            recv_sem=rim_recv.at[n],
            device_id=along(1),
            device_id_type=MESH,
        )

    def tail_copy(n, src):
        return pltpu.make_async_remote_copy(
            src_ref=src.at[pl.ds(0, head)],
            dst_ref=tails.at[n],
            send_sem=tail_send.at[n],
            recv_sem=tail_recv.at[n],
            device_id=along(TALL - 1),
            device_id_type=MESH,
        )

    first_z, last_z = z == 0, z == TALL - 1

    def before(value, outer):
        lowest = jnp.where(high, pltpu.roll(outer, 1, 0), 0.0)
        outer = jnp.where(first_z, lowest, pltpu.roll(outer, 5, 0))
        return jnp.where(step_x > 0, pltpu.roll(value, 1, 0), outer)

    def after(value, outer):
        highest = jnp.where(high, 0.0, pltpu.roll(outer, 7, 0))
        outer = jnp.where(last_z, highest, pltpu.roll(outer, 3, 0))
        return jnp.where(step_x < WIDE - 1, pltpu.roll(value, 7, 0), outer)

    def rim(n, ref):
        for j in range(reach):
            ref[fixed(j), :] = before(ref[fixed(steps + j), :], rims[n, fixed(j), :])

    def tail(n, ref):
        for j in range(reach):
            ref[fixed(steps + j), :] = after(ref[fixed(j), :], tails[n, fixed(j), :])

    def tap(stream, j):
        return entry(n_taps + stream * taps + j)

    def filtered(ref, stream, t):
        total = tap(stream, 0) * ref[at(t + reach), :]
        for j in range(1, taps):
            total = total + tap(stream, j) * ref[at(t + reach - j), :]
        return rounded(total)

    def pair_features(t, carry):
        key, value = filtered(xk, 1, t), filtered(xv, 2, t)
        ks[at(t), :] = key
        vs[at(t), :] = value
        gs[at(t), :] = rounded(key * value)
        return carry

    def query_features(t, carry):
        query = filtered(xq, 0, t)
        qs[at(t), :] = query
        us[at(t), :] = rounded(xc[at(t + reach), :] * query)
        return carry

    zero = jnp.zeros((SUBS, LANES), F32)
    zeros = tuple(zero for _ in range(modes))

    def ahead_step(t, carry):
        gated = gs[at(t), :]
        return tuple(entry(m) * carry[m] + gated for m in range(modes))

    def back_step(i, carry):
        upstream = us[at(steps - 1 - i), :]
        return tuple(entry(m) * carry[m] + upstream for m in range(modes))

    def scan_ahead(value, m):
        power = jnp.exp(logs[fixed(m), :])
        for by in (1, 2):
            value = value + power * jnp.where(step_x >= by, pltpu.roll(value, by, 0), 0.0)
            power = power * power
        return value

    def scan_back(value, m):
        power = jnp.exp(logs[fixed(m), :])
        for by in (1, 2):
            value = value + power * jnp.where(step_x < WIDE - by, pltpu.roll(value, SUBS - by, 0), 0.0)
            power = power * power
        return value

    def ahead_row(n):
        return step_x == WIDE - 1 - n

    def back_row(n):
        return step_x == n

    def finish_ends(ends, scan, store, src, row_of, sign):
        for g in range(modes // WIDE):
            packed = zero
            for n in range(WIDE):
                m = g * WIDE + n
                value = scan(ends[m], m)
                store[fixed(m), :] = value
                packed = jnp.where(row_of(n), value if n == 0 else pltpu.roll(value, (sign * n) % SUBS, 0), packed)
            src[fixed(g), :] = packed

    def seeds(store, held, row_of, sign, order, inside, leap, fresh, weight):
        for g in range(modes // WIDE):
            slow = zero
            for n in range(WIDE):
                slow = jnp.where(row_of(n), logs[fixed(g * WIDE + n), :], slow)
            far = jnp.exp(float(WIDE) * slow)
            full, part = zero, zero
            for other in order:
                value = held[other, fixed(g), :]
                full = far * full + value
                part = jnp.where(inside(other), far * part + value, part)
            part = part + jnp.where(fresh, jnp.exp(slow * leap) * pltpu.roll(full, WIDE, 0), 0.0)
            for n in range(WIDE):
                m = g * WIDE + n
                value = jnp.where(row_of(n), part, 0.0)
                if n:
                    value = pltpu.roll(value, (-sign * n) % SUBS, 0)
                value = value + pltpu.roll(value, sign % SUBS, 0)
                value = value + pltpu.roll(value, (2 * sign) % SUBS, 0)
                value = jnp.exp(logs[fixed(m), :] * weight) * value
                near = pltpu.roll(store[fixed(m), :], (-sign) % SUBS, 0)
                keep = step_x > 0 if sign < 0 else step_x < WIDE - 1
                store[fixed(m), :] = jnp.where(keep, near, 0.0) + value

    float_x = step_x.astype(F32)
    float_z = z.astype(F32)

    unpack(0, xk)
    unpack(1, xv)
    rim_copies = [rim_copy(0, xk), rim_copy(1, xv)]
    for copy in rim_copies:
        copy.start()
    lax.fori_loop(reach, steps, pair_features, 0, unroll=6)
    ends = lax.fori_loop(reach, steps, ahead_step, zeros, unroll=6)
    for copy in rim_copies:
        copy.wait()
    rim(0, xk)
    rim(1, xv)
    for t in range(reach):
        pair_features(t, 0)
    ends = list(ends)
    for m in range(modes):
        for t in range(reach):
            ends[m] = ends[m] + jnp.exp(logs[fixed(m), :] * (float(steps - 1 - t) / steps)) * gs[fixed(t), :]
    finish_ends(ends, scan_ahead, lst, fsrc, ahead_row, -1)
    unpack(2, xq)
    ahead_copy = line(fsrc, fin, 1)
    query_rim = rim_copy(2, xq)
    query_rim.start()
    unpack(3, xc)
    query_rim.wait()
    rim(2, xq)
    lax.fori_loop(0, steps, query_features, 0, unroll=4)
    ends = lax.fori_loop(0, steps, back_step, zeros, unroll=4)
    finish_ends(ends, scan_back, pst, bsrc, back_row, 1)
    back_copy = line(bsrc, bin_, 2)
    line_wait(ahead_copy, fin, 1)
    seeds(
        lst, fin, ahead_row, -1, range(TALL), lambda other: other < z, float(WIDE) * float_z, high, float_x
    )

    for group in range(0, modes, GROUP):
        members = range(group, group + GROUP)

        def forward(t, carry):
            states, firsts = carry
            gated = gs[at(t), :]
            upstream = us[at(t), :]
            total = zero if group == 0 else ys[at(t), :]
            new_s, new_f = [], []
            for n, m in enumerate(members):
                past[at(t * modes + m), :] = states[n]
                state = entry(m) * states[n] + gated
                new_f.append(firsts[n] + upstream * state)
                total = total + entry(modes + m) * state
                new_s.append(state)
            ys[at(t), :] = total
            return tuple(new_s), tuple(new_f)

        few = tuple(zero for _ in members)
        _, firsts = lax.fori_loop(0, steps, forward, (tuple(lst[fixed(m), :] for m in members), few), unroll=2)
        for n, m in enumerate(members):
            qacc[pl.ds(m, 1), :] = jnp.sum(firsts[n], axis=0, keepdims=True)

    def gradient(a, stream, t):
        total = tap(stream, 0) * a[at(t), :]
        for j in range(1, taps):
            total = total + tap(stream, j) * a[at(t + j), :]
        return total

    def pack(src, dst):
        for i in range(PLANE):
            value = src[pl.ds(i, steps, stride=SUBS), :].astype(BF16)
            dst[i] = flipped(value).astype(BF16).reshape(dst.shape[1:])

    def query_products(t, carry):
        mixed = rounded(ys[at(t), :])
        ys[at(t), :] = qs[at(t), :] * mixed
        grad = rounded(xc[at(t + reach), :] * mixed)
        aq[at(t), :] = grad
        return tuple(carry[j] + grad * xq[at(t + reach - j), :] for j in range(taps))

    def query_gradients(t, carry):
        ss[at(t), :] = gradient(aq, 0, t)
        return carry

    results, outputs = (oo, oq, ok, ov), (out_ref, dq_ref, dk_ref, dv_ref)
    kept_out = []

    def deliver(n):
        for step in range(1, PLANE):
            s, peer = across(step)
            pltpu.make_async_remote_copy(
                src_ref=results[n].at[s],
                dst_ref=outputs[n].at[y, :, x],
                send_sem=out_send.at[n],
                recv_sem=out_recv.at[n],
                device_id=peer,
                device_id_type=MESH,
            ).start()
        copy = pltpu.make_async_copy(results[n].at[spot], outputs[n].at[y, :, x], keep_sem.at[4 + n])
        copy.start()
        kept_out.append(copy)

    sums = lax.fori_loop(0, steps, query_products, tuple(zero for _ in range(taps)), unroll=2)
    for n in range(taps):
        tacc[pl.ds(n, 1), :] = jnp.sum(sums[n], axis=0, keepdims=True)
    query_tail = tail_copy(0, aq)
    query_tail.start()
    pack(ys, oo)
    query_tail.wait()
    tail(0, aq)
    deliver(0)
    lax.fori_loop(0, steps, query_gradients, 0, unroll=4)
    pack(ss, oq)
    line_wait(back_copy, bin_, 2)
    seeds(
        pst, bin_, back_row, 1, range(TALL - 1, -1, -1), lambda other: other > z,
        float(WIDE) * (float(TALL - 1) - float_z), jnp.logical_not(high), float(WIDE - 1) - float_x,
    )
    deliver(1)

    for group in range(0, modes, GROUP):
        members = range(group, group + GROUP)

        def backward(i, carry):
            states, seconds = carry
            t = steps - 1 - i
            upstream = us[at(t), :]
            total = zero if group == 0 else ss[at(t), :]
            new_s, new_r = [], []
            for n, m in enumerate(members):
                state = entry(m) * states[n] + upstream
                new_r.append(seconds[n] + state * past[at(t * modes + m), :])
                total = total + entry(modes + m) * state
                new_s.append(state)
            ss[at(t), :] = total
            return tuple(new_s), tuple(new_r)

        few = tuple(zero for _ in members)
        _, seconds = lax.fori_loop(0, steps, backward, (tuple(pst[fixed(m), :] for m in members), few), unroll=2)
        for n, m in enumerate(members):
            racc[pl.ds(m, 1), :] = jnp.sum(seconds[n], axis=0, keepdims=True)

    def pair_products(t, carry):
        source = rounded(ss[at(t), :])
        new = []
        for n, (other, ref, x_ref) in enumerate(((vs, ak, xk), (ks, av, xv))):
            grad = rounded(source * other[at(t), :])
            ref[at(t), :] = grad
            for j in range(taps):
                new.append(carry[n * taps + j] + grad * x_ref[at(t + reach - j), :])
        return tuple(new)

    def pair_gradients(t, carry):
        ys[at(t), :] = gradient(ak, 1, t)
        ss[at(t), :] = gradient(av, 2, t)
        return carry

    sums = lax.fori_loop(0, steps, pair_products, tuple(zero for _ in range(2 * taps)), unroll=2)
    for n in range(2 * taps):
        tacc[pl.ds(taps + n, 1), :] = jnp.sum(sums[n], axis=0, keepdims=True)
    tail_copies = [tail_copy(1, ak), tail_copy(2, av)]
    for copy in tail_copies:
        copy.start()
    tap_part[...] = scale * tacc[...]
    first, second = qacc[...], racc[...] * damp
    mode_part[pl.ds(0, modes), :] = scale * size * first
    mode_part[pl.ds(modes, modes), :] = (
        scale * rate * (residue * (damp * damp / size) * first - weighted * second)
    )
    tap_copy = line(tap_part, tap_stack, 3)
    mode_copy = line(mode_part, mode_stack, 4)
    lax.fori_loop(0, steps - reach, pair_gradients, 0, unroll=6)
    for copy in tail_copies:
        copy.wait()
    tail(1, ak)
    tail(2, av)
    for t in range(steps - reach, steps):
        pair_gradients(t, 0)
    pack(ys, ok)
    pack(ss, ov)
    deliver(2)
    deliver(3)

    def summed(ref, count):
        total = ref[0]
        for n in range(1, count):
            total = total + ref[n]
        return total

    def pairs_of(ref, base):
        local = pltpu.make_async_copy(ref.at[doubles], ref.at[mine], keep_sem.at[13 + base])
        copies = [
            pltpu.make_async_remote_copy(
                src_ref=ref.at[doubles],
                dst_ref=ref.at[mine],
                send_sem=pair_send.at[base * doubles + step],
                recv_sem=pair_recv.at[base * doubles + step],
                device_id={"dp": lax.rem(mine + step, doubles)},
                device_id_type=MESH,
            )
            for step in range(1, doubles)
        ]
        for copy in copies + [local]:
            copy.start()
        return copies + [local]

    line_wait(tap_copy, tap_stack, 3)
    tap_slots[doubles] = summed(tap_stack, TALL)
    tap_pairs = pairs_of(tap_slots, 0)
    line_wait(mode_copy, mode_stack, 4)
    mode_slots[doubles] = summed(mode_stack, TALL)
    for pair in tap_pairs:
        pair.wait()
    total_ref[...] = summed(tap_slots, doubles)
    mode_pairs = pairs_of(mode_slots, 1)
    for step in range(1, PLANE):
        pltpu.make_async_remote_copy(
            src_ref=total_ref,
            dst_ref=shared_ref.at[spot],
            send_sem=tap_send,
            recv_sem=tap_recv,
            device_id=across(step)[1],
            device_id_type=MESH,
        ).start()
    own_taps = pltpu.make_async_copy(total_ref, shared_ref.at[spot], keep_sem.at[15])
    own_taps.start()
    for pair in mode_pairs:
        pair.wait()
    total = summed(mode_slots, doubles)
    for ref, start in ((dres_ref, 0), (drate_ref, modes)):
        ref[...] = lax.dot_general(
            mine_lanes,
            total[start : start + modes],
            (((1,), (1,)), ((), ())),
            precision=HIGHEST,
            preferred_element_type=F32,
        )
    for n in range(4):
        settle(landed[n].at[pl.ds(0, PLANE - 1)], in_send.at[n])
    for copy in kept_out:
        copy.wait()
    own_taps.wait()
    for n in range(4):
        settle(results[n].at[pl.ds(0, PLANE - 1)], out_send.at[n])
        settle(outputs[n].at[:, pl.ds(0, TALL - 1)], out_recv.at[n])
    settle(shared_ref.at[pl.ds(0, PLANE - 1)], tap_send, tap_recv)


def closing_kernel(own, taps, *refs):
    sources, shared_ref, parts, targets = refs[:4], refs[4], refs[5:7], refs[7:11]
    taps_ref, finals = refs[11], refs[12:]
    for source, target in zip(sources, targets):
        target[0] = source[...].reshape(target.shape[1:])
    for part, final in zip(parts, finals):
        final[...] = part[...]
    rows = shared_ref.shape[1]
    group = lax.broadcasted_iota(jnp.int32, (rows, LANES), 1) // own
    groups = LANES // own
    for b in range(taps_ref.shape[2] // LANES):
        y, pair = b // WIDE, b % WIDE
        value = jnp.zeros((rows, LANES), F32)
        for spot in range(groups):
            z, x = pair * (groups // WIDE) + spot // WIDE, spot % WIDE
            held = shared_ref[y * WIDE + x]
            held = pltpu.roll(held, (spot - z) * own % LANES, 1)
            value = jnp.where(group == spot, held, value)
        for stream in range(3):
            taps_ref[stream, :, pl.ds(b * LANES, LANES)] = value[stream * taps : (stream + 1) * taps]


def per_device(queries, key_stream, value_stream, cotangent, short_taps, residues, decay_rates):
    channels, steps = queries.shape[1], queries.shape[2]
    own, modes = residues.shape
    taps = short_taps.shape[1]
    owners, doubles = lax.axis_size("context"), lax.axis_size("dp")
    scale = 1.0 / math.sqrt(queries.shape[0] * doubles * steps * owners)
    view = (owners // (TALL * WIDE), TALL, WIDE, own, steps)
    wide = jax.ShapeDtypeStruct(view, BF16)
    mode_shape = jax.ShapeDtypeStruct(residues.shape, F32)
    line, reach = steps * SUBS, taps - 1
    vm = pltpu.VMEM
    here = pl.BlockSpec(memory_space=vm)
    away = pl.BlockSpec(memory_space=pl.ANY)
    dma = pltpu.SemaphoreType.DMA
    tap_rows = -(-3 * taps // SUBS) * SUBS
    ends = modes // WIDE * SUBS
    streams = [x.reshape(view) for x in (queries, key_stream, value_stream, cotangent)]
    results = pl.pallas_call(
        functools.partial(operator_kernel, modes, taps, steps, doubles, scale),
        out_shape=[wide] * 4 + [jax.ShapeDtypeStruct((PLANE, tap_rows, LANES), F32), mode_shape, mode_shape],
        in_specs=[away] * 4 + [here] * 3,
        out_specs=[away] * 4 + [here] * 3,
        scratch_shapes=[vm((PLANE, TALL, own, steps), BF16)] * 8
        + [vm((line + reach * SUBS, LANES), F32)] * 4
        + [vm((line, LANES), F32)] * 7
        + [vm((line + reach * SUBS, LANES), F32)] * 3
        + [
            vm(((2 * modes + 3 * taps) * SUBS, LANES), F32),
            vm((modes * SUBS, LANES), F32),
            vm((modes * SUBS, LANES), F32),
            vm((modes * SUBS, LANES), F32),
            vm((line * modes, LANES), F32),
            vm((modes, LANES), F32),
            vm((modes, LANES), F32),
            vm((tap_rows, LANES), F32),
            vm((2 * modes, LANES), F32),
            vm((TALL, 2 * modes, LANES), F32),
            vm((ends, LANES), F32),
            vm((TALL, ends, LANES), F32),
            vm((ends, LANES), F32),
            vm((TALL, ends, LANES), F32),
            vm((3, reach * SUBS, LANES), F32),
            vm((3, reach * SUBS, LANES), F32),
            vm((tap_rows, LANES), F32),
            vm((TALL, tap_rows, LANES), F32),
            vm((doubles + 1, tap_rows, LANES), F32),
            vm((2 * modes, LANES), F32),
            vm((TALL, 2 * modes, LANES), F32),
            vm((doubles + 1, 2 * modes, LANES), F32),
            vm((tap_rows, LANES), F32),
        ]
        + [dma((4,))] * 4
        + [dma((16,)), dma((2 * doubles,)), dma((2 * doubles,))]
        + [dma((3,))] * 4
        + [dma((5,))] * 2
        + [dma, dma],
        compiler_params=pltpu.CompilerParams(collective_id=0, has_side_effects=True),
    )(*streams, short_taps, residues, decay_rates)
    return pl.pallas_call(
        functools.partial(closing_kernel, own, taps),
        out_shape=[jax.ShapeDtypeStruct(queries.shape, BF16)] * 4
        + [jax.ShapeDtypeStruct(short_taps.shape, F32), mode_shape, mode_shape],
        in_specs=[here] * 7,
        out_specs=[here] * 7,
    )(*results)


def solution(mesh):
    stream = P("dp", None, "context")
    in_specs = (stream,) * 4 + (P(), P("context", None), P("context", None))
    out_specs = (stream,) * 4 + (P(), P("context", None), P("context", None))
    return jax.shard_map(per_device, mesh=mesh, in_specs=in_specs, out_specs=out_specs, check_vma=False)
```

```python
import functools
import math

import jax
import jax.numpy as jnp
from jax import lax
from jax.experimental import pallas as pl
from jax.experimental.pallas import tpu as pltpu
from jax.sharding import PartitionSpec as P

F32 = jnp.float32
BF16 = jnp.bfloat16
HIGHEST = lax.Precision.HIGHEST
LANES = 128
SUBS = 8
GROUP = 16
TALL = 8
WIDE = 4
PLANE = 8
PAIR = 2


def rounded(x):
    return x.astype(BF16).astype(F32)


MESH = pl.DeviceIdType.MESH


def place(index):
    return index // (TALL * WIDE), lax.rem(index // WIDE, TALL), lax.rem(index, WIDE)


def context_of(y, z, x):
    return (y * TALL + z) * WIDE + x


def settle(ref, send, recv=None):
    pltpu.make_async_copy(ref, ref, send).wait()
    if recv is not None:
        pltpu.make_async_copy(ref, ref, recv).wait()


def operator_kernel(
    modes, taps, steps, doubles, scale,
    q_ref, k_ref, v_ref, c_ref, taps_ref, residue_ref, rate_ref,
    out_ref, dq_ref, dk_ref, dv_ref, shared_ref, dres_ref, drate_ref,
    mq, mk, mv, mc, oo, oq, ok, ov,
    xq, xk, xv, xc, qs, ks, vs, gs, us, ys, ss, aq, ak, av,
    tab, logs, lst, pst, past, qacc, racc, tacc,
    tsrc, tin, fsrc, fin, bsrc, bin_, rims, tails,
    tap_part, tap_stack, mode_part, mode_stack, mode_slots, total_ref,
    in_send, in_recv, out_send, out_recv, keep_sem, pair_send, pair_recv,
    rim_send, rim_recv, tail_send, tail_recv, line_send, line_recv, tap_send, tap_recv,
):
    y, z, x = place(lax.axis_index("context"))
    mine = lax.axis_index("dp")
    spot = y * WIDE + x
    own = residue_ref.shape[0]
    barrier = pltpu.get_barrier_semaphore()

    def across(step):
        s = lax.rem(spot + step, PLANE)
        return s, {"context": context_of(s // WIDE, z, lax.rem(s, WIDE))}

    def along(step):
        return {"context": context_of(y, lax.rem(z + step, TALL), x)}

    outer, inner = mine // PAIR, lax.rem(mine, PAIR)
    tower, field = z * PAIR + inner, spot * PAIR + outer

    def in_tower(step):
        q = lax.rem(tower + step, TALL * PAIR)
        return {"dp": outer * PAIR + lax.rem(q, PAIR), "context": context_of(y, q // PAIR, x)}

    def in_field(step):
        q = lax.rem(field + step, PLANE * PAIR)
        s = q // PAIR
        return {
            "dp": lax.rem(q, PAIR) * PAIR + inner,
            "context": context_of(s // WIDE, z, lax.rem(s, WIDE)),
        }

    for step in range(1, TALL * PAIR):
        pl.semaphore_signal(barrier, inc=1, device_id=in_tower(step), device_id_type=MESH)
    for step in range(1, PLANE * PAIR):
        pl.semaphore_signal(barrier, inc=1, device_id=in_field(step), device_id_type=MESH)
    pl.semaphore_signal(barrier, inc=1, device_id={"dp": doubles - 1 - mine}, device_id_type=MESH)

    sources, landed = (k_ref, v_ref, q_ref, c_ref), (mk, mv, mq, mc)
    kept = [
        pltpu.make_async_copy(sources[n].at[y, :, x], landed[n].at[spot], keep_sem.at[n]) for n in range(4)
    ]
    for copy in kept:
        copy.start()

    lane = lax.broadcasted_iota(jnp.int32, (SUBS, LANES), 1)
    sub = lax.broadcasted_iota(jnp.int32, (SUBS, LANES), 0)
    step_x = lax.rem(sub, WIDE)
    high = sub >= WIDE

    def at(t):
        return pl.ds(pl.multiple_of(t * SUBS, SUBS), SUBS)

    def fixed(row):
        return pl.ds(row * SUBS, SUBS)

    mine_lanes = (
        lax.broadcasted_iota(jnp.int32, (own, LANES), 1)
        == z * own + lax.broadcasted_iota(jnp.int32, (own, LANES), 0)
    ).astype(F32)
    turn = (((0,), (0,)), ((), ()))
    tsrc[pl.ds(0, modes), :] = lax.dot_general(
        residue_ref[...], mine_lanes, turn, precision=HIGHEST, preferred_element_type=F32
    )
    tsrc[pl.ds(modes, modes), :] = lax.dot_general(
        rate_ref[...], mine_lanes, turn, precision=HIGHEST, preferred_element_type=F32
    )
    half = taps_ref.shape[2] // 2
    column = lax.broadcasted_iota(jnp.int32, (half, LANES), 1)
    chosen = (
        lax.broadcasted_iota(jnp.int32, (half, LANES), 0)
        == column // own * (WIDE * own) + x * own + lax.rem(column, own)
    ).astype(F32)
    block = pl.ds(pl.multiple_of(y * half, half), half)
    n_taps = 2 * modes
    for stream in range(3):
        picked = jnp.dot(taps_ref[stream, :, block], chosen, precision=HIGHEST, preferred_element_type=F32)
        for j in range(taps):
            tab[fixed(n_taps + stream * taps + j), :] = jnp.broadcast_to(picked[j : j + 1, :], (SUBS, LANES))
    tacc[...] = jnp.zeros(tacc.shape, F32)

    def line(src, dst, n):
        for step in range(1, TALL):
            pltpu.make_async_remote_copy(
                src_ref=src,
                dst_ref=dst.at[z],
                send_sem=line_send.at[n],
                recv_sem=line_recv.at[n],
                device_id=along(step),
                device_id_type=MESH,
            ).start()
        copy = pltpu.make_async_copy(src, dst.at[z], keep_sem.at[8 + n])
        copy.start()
        return copy

    def line_wait(copy, dst, n):
        copy.wait()
        settle(dst.at[pl.ds(0, TALL - 1)], line_send.at[n], line_recv.at[n])

    pl.semaphore_wait(barrier, TALL * PAIR + PLANE * PAIR - 1)
    table_copy = line(tsrc, tin, 0)
    for n in range(4):
        for step in range(1, PLANE):
            s, peer = across(step)
            pltpu.make_async_remote_copy(
                src_ref=sources[n].at[s // WIDE, :, lax.rem(s, WIDE)],
                dst_ref=landed[n].at[spot],
                send_sem=in_send.at[n],
                recv_sem=in_recv.at[n],
                device_id=peer,
                device_id_type=MESH,
            ).start()

    line_wait(table_copy, tin, 0)
    tables = tin[0]
    for n in range(1, TALL):
        tables = tables + tin[n]
    residue, rate = tables[:modes], tables[modes:]
    double = 2.0 * rate
    series = 1.0 - double / 7.0
    for n in range(6, 1, -1):
        series = 1.0 - double / float(n) * series
    size = jnp.sqrt(double * series)
    damp = jnp.exp(-rate)
    weighted = residue * size
    for m in range(modes):
        tab[fixed(m), :] = jnp.broadcast_to(damp[m : m + 1, :], (SUBS, LANES))
        tab[fixed(modes + m), :] = jnp.broadcast_to(weighted[m : m + 1, :], (SUBS, LANES))
        logs[fixed(m), :] = jnp.broadcast_to(-float(steps) * rate[m : m + 1, :], (SUBS, LANES))

    def entry(row):
        return tab[fixed(row), :]

    ones = (
        lax.broadcasted_iota(jnp.int32, (LANES, LANES), 0)
        == lax.broadcasted_iota(jnp.int32, (LANES, LANES), 1)
    ).astype(BF16)

    def flipped(value):
        return lax.dot_general(ones, value, (((1,), (1,)), ((), ())), preferred_element_type=F32)

    reach = taps - 1
    head = reach * SUBS

    def unpack(n, dst):
        kept[n].wait()
        settle(landed[n].at[pl.ds(0, PLANE - 1)], in_recv.at[n])
        for i in range(PLANE):
            dst[pl.ds(head + i, steps, stride=SUBS), :] = flipped(landed[n][i].reshape(LANES, steps))

    def rim_copy(n, src):
        return pltpu.make_async_remote_copy(
            src_ref=src.at[pl.ds(steps * SUBS, head)],
            dst_ref=rims.at[n],
            send_sem=rim_send.at[n],
            recv_sem=rim_recv.at[n],
            device_id=along(1),
            device_id_type=MESH,
        )

    def tail_copy(n, src):
        return pltpu.make_async_remote_copy(
            src_ref=src.at[pl.ds(0, head)],
            dst_ref=tails.at[n],
            send_sem=tail_send.at[n],
            recv_sem=tail_recv.at[n],
            device_id=along(TALL - 1),
            device_id_type=MESH,
        )

    first_z, last_z = z == 0, z == TALL - 1

    def before(value, outer):
        lowest = jnp.where(high, pltpu.roll(outer, 1, 0), 0.0)
        outer = jnp.where(first_z, lowest, pltpu.roll(outer, 5, 0))
        return jnp.where(step_x > 0, pltpu.roll(value, 1, 0), outer)

    def after(value, outer):
        highest = jnp.where(high, 0.0, pltpu.roll(outer, 7, 0))
        outer = jnp.where(last_z, highest, pltpu.roll(outer, 3, 0))
        return jnp.where(step_x < WIDE - 1, pltpu.roll(value, 7, 0), outer)

    def rim(n, ref):
        for j in range(reach):
            ref[fixed(j), :] = before(ref[fixed(steps + j), :], rims[n, fixed(j), :])

    def tail(n, ref):
        for j in range(reach):
            ref[fixed(steps + j), :] = after(ref[fixed(j), :], tails[n, fixed(j), :])

    def tap(stream, j):
        return entry(n_taps + stream * taps + j)

    def filtered(ref, stream, t):
        total = tap(stream, 0) * ref[at(t + reach), :]
        for j in range(1, taps):
            total = total + tap(stream, j) * ref[at(t + reach - j), :]
        return rounded(total)

    def pair_features(t, carry):
        key, value = filtered(xk, 1, t), filtered(xv, 2, t)
        ks[at(t), :] = key
        vs[at(t), :] = value
        gs[at(t), :] = rounded(key * value)
        return carry

    def query_features(t, carry):
        query = filtered(xq, 0, t)
        qs[at(t), :] = query
        us[at(t), :] = rounded(xc[at(t + reach), :] * query)
        return carry

    zero = jnp.zeros((SUBS, LANES), F32)
    zeros = tuple(zero for _ in range(modes))

    def ahead_step(t, carry):
        gated = gs[at(t), :]
        return tuple(entry(m) * carry[m] + gated for m in range(modes))

    def back_step(i, carry):
        upstream = us[at(steps - 1 - i), :]
        return tuple(entry(m) * carry[m] + upstream for m in range(modes))

    def scan_ahead(value, m):
        power = jnp.exp(logs[fixed(m), :])
        for by in (1, 2):
            value = value + power * jnp.where(step_x >= by, pltpu.roll(value, by, 0), 0.0)
            power = power * power
        return value

    def scan_back(value, m):
        power = jnp.exp(logs[fixed(m), :])
        for by in (1, 2):
            value = value + power * jnp.where(step_x < WIDE - by, pltpu.roll(value, SUBS - by, 0), 0.0)
            power = power * power
        return value

    def ahead_row(n):
        return step_x == WIDE - 1 - n

    def back_row(n):
        return step_x == n

    def finish_ends(ends, scan, store, src, row_of, sign):
        for g in range(modes // WIDE):
            packed = zero
            for n in range(WIDE):
                m = g * WIDE + n
                value = scan(ends[m], m)
                store[fixed(m), :] = value
                packed = jnp.where(row_of(n), value if n == 0 else pltpu.roll(value, (sign * n) % SUBS, 0), packed)
            src[fixed(g), :] = packed

    def seeds(store, held, row_of, sign, order, inside, leap, fresh, weight):
        for g in range(modes // WIDE):
            slow = zero
            for n in range(WIDE):
                slow = jnp.where(row_of(n), logs[fixed(g * WIDE + n), :], slow)
            far = jnp.exp(float(WIDE) * slow)
            full, part = zero, zero
            for other in order:
                value = held[other, fixed(g), :]
                full = far * full + value
                part = jnp.where(inside(other), far * part + value, part)
            part = part + jnp.where(fresh, jnp.exp(slow * leap) * pltpu.roll(full, WIDE, 0), 0.0)
            for n in range(WIDE):
                m = g * WIDE + n
                value = jnp.where(row_of(n), part, 0.0)
                if n:
                    value = pltpu.roll(value, (-sign * n) % SUBS, 0)
                value = value + pltpu.roll(value, sign % SUBS, 0)
                value = value + pltpu.roll(value, (2 * sign) % SUBS, 0)
                value = jnp.exp(logs[fixed(m), :] * weight) * value
                near = pltpu.roll(store[fixed(m), :], (-sign) % SUBS, 0)
                keep = step_x > 0 if sign < 0 else step_x < WIDE - 1
                store[fixed(m), :] = jnp.where(keep, near, 0.0) + value

    float_x = step_x.astype(F32)
    float_z = z.astype(F32)

    unpack(0, xk)
    unpack(1, xv)
    rim_copies = [rim_copy(0, xk), rim_copy(1, xv)]
    for copy in rim_copies:
        copy.start()
    lax.fori_loop(reach, steps, pair_features, 0, unroll=6)
    ends = lax.fori_loop(reach, steps, ahead_step, zeros, unroll=6)
    for copy in rim_copies:
        copy.wait()
    rim(0, xk)
    rim(1, xv)
    for t in range(reach):
        pair_features(t, 0)
    ends = list(ends)
    for m in range(modes):
        for t in range(reach):
            ends[m] = ends[m] + jnp.exp(logs[fixed(m), :] * (float(steps - 1 - t) / steps)) * gs[fixed(t), :]
    finish_ends(ends, scan_ahead, lst, fsrc, ahead_row, -1)
    unpack(2, xq)
    ahead_copy = line(fsrc, fin, 1)
    query_rim = rim_copy(2, xq)
    query_rim.start()
    unpack(3, xc)
    query_rim.wait()
    rim(2, xq)
    lax.fori_loop(0, steps, query_features, 0, unroll=4)
    ends = lax.fori_loop(0, steps, back_step, zeros, unroll=4)
    finish_ends(ends, scan_back, pst, bsrc, back_row, 1)
    back_copy = line(bsrc, bin_, 2)
    line_wait(ahead_copy, fin, 1)
    seeds(
        lst, fin, ahead_row, -1, range(TALL), lambda other: other < z, float(WIDE) * float_z, high, float_x
    )

    for group in range(0, modes, GROUP):
        members = range(group, group + GROUP)

        def forward(t, carry):
            states, firsts = carry
            gated = gs[at(t), :]
            upstream = us[at(t), :]
            total = zero if group == 0 else ys[at(t), :]
            new_s, new_f = [], []
            for n, m in enumerate(members):
                past[at(t * modes + m), :] = states[n]
                state = entry(m) * states[n] + gated
                new_f.append(firsts[n] + upstream * state)
                total = total + entry(modes + m) * state
                new_s.append(state)
            ys[at(t), :] = total
            return tuple(new_s), tuple(new_f)

        few = tuple(zero for _ in members)
        _, firsts = lax.fori_loop(0, steps, forward, (tuple(lst[fixed(m), :] for m in members), few), unroll=4)
        for n, m in enumerate(members):
            qacc[pl.ds(m, 1), :] = jnp.sum(firsts[n], axis=0, keepdims=True)

    def gradient(a, stream, t):
        total = tap(stream, 0) * a[at(t), :]
        for j in range(1, taps):
            total = total + tap(stream, j) * a[at(t + j), :]
        return total

    def pack(src, dst):
        for i in range(PLANE):
            value = src[pl.ds(i, steps, stride=SUBS), :].astype(BF16)
            dst[i] = flipped(value).astype(BF16).reshape(dst.shape[1:])

    def query_products(t, carry):
        mixed = rounded(ys[at(t), :])
        ys[at(t), :] = qs[at(t), :] * mixed
        grad = rounded(xc[at(t + reach), :] * mixed)
        aq[at(t), :] = grad
        return tuple(carry[j] + grad * xq[at(t + reach - j), :] for j in range(taps))

    def query_gradients(t, carry):
        ss[at(t), :] = gradient(aq, 0, t)
        return carry

    results, outputs = (oo, oq, ok, ov), (out_ref, dq_ref, dk_ref, dv_ref)
    kept_out = []

    def deliver(n):
        for step in range(1, PLANE):
            s, peer = across(step)
            pltpu.make_async_remote_copy(
                src_ref=results[n].at[s],
                dst_ref=outputs[n].at[y, :, x],
                send_sem=out_send.at[n],
                recv_sem=out_recv.at[n],
                device_id=peer,
                device_id_type=MESH,
            ).start()
        copy = pltpu.make_async_copy(results[n].at[spot], outputs[n].at[y, :, x], keep_sem.at[4 + n])
        copy.start()
        kept_out.append(copy)

    sums = lax.fori_loop(0, steps, query_products, tuple(zero for _ in range(taps)), unroll=4)
    for n in range(taps):
        tacc[pl.ds(n, 1), :] = jnp.sum(sums[n], axis=0, keepdims=True)
    query_tail = tail_copy(0, aq)
    query_tail.start()
    pack(ys, oo)
    query_tail.wait()
    tail(0, aq)
    deliver(0)
    lax.fori_loop(0, steps, query_gradients, 0, unroll=4)
    pack(ss, oq)
    line_wait(back_copy, bin_, 2)
    seeds(
        pst, bin_, back_row, 1, range(TALL - 1, -1, -1), lambda other: other > z,
        float(WIDE) * (float(TALL - 1) - float_z), jnp.logical_not(high), float(WIDE - 1) - float_x,
    )
    deliver(1)

    for group in range(0, modes, GROUP):
        members = range(group, group + GROUP)

        def backward(i, carry):
            states, seconds = carry
            t = steps - 1 - i
            upstream = us[at(t), :]
            total = zero if group == 0 else ss[at(t), :]
            new_s, new_r = [], []
            for n, m in enumerate(members):
                state = entry(m) * states[n] + upstream
                new_r.append(seconds[n] + state * past[at(t * modes + m), :])
                total = total + entry(modes + m) * state
                new_s.append(state)
            ss[at(t), :] = total
            return tuple(new_s), tuple(new_r)

        few = tuple(zero for _ in members)
        _, seconds = lax.fori_loop(0, steps, backward, (tuple(pst[fixed(m), :] for m in members), few), unroll=4)
        for n, m in enumerate(members):
            racc[pl.ds(m, 1), :] = jnp.sum(seconds[n], axis=0, keepdims=True)

    def pair_products(t, carry):
        source = rounded(ss[at(t), :])
        new = []
        for n, (other, ref, x_ref) in enumerate(((vs, ak, xk), (ks, av, xv))):
            grad = rounded(source * other[at(t), :])
            ref[at(t), :] = grad
            for j in range(taps):
                new.append(carry[n * taps + j] + grad * x_ref[at(t + reach - j), :])
        return tuple(new)

    def pair_gradients(t, carry):
        ys[at(t), :] = gradient(ak, 1, t)
        ss[at(t), :] = gradient(av, 2, t)
        return carry

    sums = lax.fori_loop(0, steps, pair_products, tuple(zero for _ in range(2 * taps)), unroll=4)
    for n in range(2 * taps):
        tacc[pl.ds(taps + n, 1), :] = jnp.sum(sums[n], axis=0, keepdims=True)
    tail_copies = [tail_copy(1, ak), tail_copy(2, av)]
    for copy in tail_copies:
        copy.start()
    tap_part[...] = scale * tacc[...]
    first, second = qacc[...], racc[...] * damp
    mode_part[pl.ds(0, modes), :] = scale * size * first
    mode_part[pl.ds(modes, modes), :] = (
        scale * rate * (residue * (damp * damp / size) * first - weighted * second)
    )
    for step in range(1, TALL * PAIR):
        pltpu.make_async_remote_copy(
            src_ref=tap_part,
            dst_ref=tap_stack.at[tower],
            send_sem=line_send.at[3],
            recv_sem=line_recv.at[3],
            device_id=in_tower(step),
            device_id_type=MESH,
        ).start()
    tap_copy = pltpu.make_async_copy(tap_part, tap_stack.at[tower], keep_sem.at[11])
    tap_copy.start()
    mode_copy = line(mode_part, mode_stack, 4)
    lax.fori_loop(0, steps - reach, pair_gradients, 0, unroll=6)
    for copy in tail_copies:
        copy.wait()
    tail(1, ak)
    tail(2, av)
    for t in range(steps - reach, steps):
        pair_gradients(t, 0)
    pack(ys, ok)
    pack(ss, ov)
    deliver(2)
    deliver(3)

    def summed(ref, count):
        total = ref[0]
        for n in range(1, count):
            total = total + ref[n]
        return total

    tap_copy.wait()
    settle(tap_stack.at[pl.ds(0, TALL * PAIR - 1)], line_send.at[3], line_recv.at[3])
    total_ref[...] = summed(tap_stack, TALL * PAIR)
    for step in range(1, PLANE * PAIR):
        pltpu.make_async_remote_copy(
            src_ref=total_ref,
            dst_ref=shared_ref.at[field],
            send_sem=tap_send,
            recv_sem=tap_recv,
            device_id=in_field(step),
            device_id_type=MESH,
        ).start()
    own_taps = pltpu.make_async_copy(total_ref, shared_ref.at[field], keep_sem.at[15])
    own_taps.start()
    line_wait(mode_copy, mode_stack, 4)
    mode_slots[doubles] = summed(mode_stack, TALL)
    mode_pairs = [
        pltpu.make_async_remote_copy(
            src_ref=mode_slots.at[doubles],
            dst_ref=mode_slots.at[mine],
            send_sem=pair_send.at[step],
            recv_sem=pair_recv.at[step],
            device_id={"dp": lax.rem(mine + step, doubles)},
            device_id_type=MESH,
        )
        for step in range(1, doubles)
    ]
    mode_pairs.append(pltpu.make_async_copy(mode_slots.at[doubles], mode_slots.at[mine], keep_sem.at[13]))
    for pair in mode_pairs:
        pair.start()
    for pair in mode_pairs:
        pair.wait()
    total = summed(mode_slots, doubles)
    for ref, start in ((dres_ref, 0), (drate_ref, modes)):
        ref[...] = lax.dot_general(
            mine_lanes,
            total[start : start + modes],
            (((1,), (1,)), ((), ())),
            precision=HIGHEST,
            preferred_element_type=F32,
        )
    for n in range(4):
        settle(landed[n].at[pl.ds(0, PLANE - 1)], in_send.at[n])
    for copy in kept_out:
        copy.wait()
    own_taps.wait()
    for n in range(4):
        settle(results[n].at[pl.ds(0, PLANE - 1)], out_send.at[n])
        settle(outputs[n].at[:, pl.ds(0, TALL - 1)], out_recv.at[n])
    settle(shared_ref.at[pl.ds(0, PLANE * PAIR - 1)], tap_send, tap_recv)


def closing_kernel(own, taps, *refs):
    sources, shared_ref, parts, targets = refs[:4], refs[4], refs[5:7], refs[7:11]
    taps_ref, finals = refs[11], refs[12:]
    for source, target in zip(sources, targets):
        target[0] = source[...].reshape(target.shape[1:])
    for part, final in zip(parts, finals):
        final[...] = part[...]
    rows = shared_ref.shape[1]
    group = lax.broadcasted_iota(jnp.int32, (rows, LANES), 1) // own
    groups = LANES // own
    for b in range(taps_ref.shape[2] // LANES):
        y, pair = b // WIDE, b % WIDE
        value = jnp.zeros((rows, LANES), F32)
        for spot in range(groups):
            z, x = pair * (groups // WIDE) + spot // WIDE, spot % WIDE
            first = (y * WIDE + x) * PAIR
            held = shared_ref[first] + shared_ref[first + 1]
            held = pltpu.roll(held, (spot - z) * own % LANES, 1)
            value = jnp.where(group == spot, held, value)
        for stream in range(3):
            taps_ref[stream, :, pl.ds(b * LANES, LANES)] = value[stream * taps : (stream + 1) * taps]


def per_device(queries, key_stream, value_stream, cotangent, short_taps, residues, decay_rates):
    channels, steps = queries.shape[1], queries.shape[2]
    own, modes = residues.shape
    taps = short_taps.shape[1]
    owners, doubles = lax.axis_size("context"), lax.axis_size("dp")
    scale = 1.0 / math.sqrt(queries.shape[0] * doubles * steps * owners)
    view = (owners // (TALL * WIDE), TALL, WIDE, own, steps)
    wide = jax.ShapeDtypeStruct(view, BF16)
    mode_shape = jax.ShapeDtypeStruct(residues.shape, F32)
    line, reach = steps * SUBS, taps - 1
    vm = pltpu.VMEM
    here = pl.BlockSpec(memory_space=vm)
    away = pl.BlockSpec(memory_space=pl.ANY)
    dma = pltpu.SemaphoreType.DMA
    tap_rows = 3 * taps
    ends = modes // WIDE * SUBS
    streams = [x.reshape(view) for x in (queries, key_stream, value_stream, cotangent)]
    results = pl.pallas_call(
        functools.partial(operator_kernel, modes, taps, steps, doubles, scale),
        out_shape=[wide] * 4 + [jax.ShapeDtypeStruct((PLANE * PAIR, tap_rows, LANES), F32), mode_shape, mode_shape],
        in_specs=[away] * 4 + [here] * 3,
        out_specs=[away] * 4 + [here] * 3,
        scratch_shapes=[vm((PLANE, TALL, own, steps), BF16)] * 8
        + [vm((line + reach * SUBS, LANES), F32)] * 4
        + [vm((line, LANES), F32)] * 7
        + [vm((line + reach * SUBS, LANES), F32)] * 3
        + [
            vm(((2 * modes + 3 * taps) * SUBS, LANES), F32),
            vm((modes * SUBS, LANES), F32),
            vm((modes * SUBS, LANES), F32),
            vm((modes * SUBS, LANES), F32),
            vm((line * modes, LANES), F32),
            vm((modes, LANES), F32),
            vm((modes, LANES), F32),
            vm((tap_rows, LANES), F32),
            vm((2 * modes, LANES), F32),
            vm((TALL, 2 * modes, LANES), F32),
            vm((ends, LANES), F32),
            vm((TALL, ends, LANES), F32),
            vm((ends, LANES), F32),
            vm((TALL, ends, LANES), F32),
            vm((3, reach * SUBS, LANES), F32),
            vm((3, reach * SUBS, LANES), F32),
            vm((tap_rows, LANES), F32),
            vm((TALL * PAIR, tap_rows, LANES), F32),
            vm((2 * modes, LANES), F32),
            vm((TALL, 2 * modes, LANES), F32),
            vm((doubles + 1, 2 * modes, LANES), F32),
            vm((tap_rows, LANES), F32),
        ]
        + [dma((4,))] * 4
        + [dma((16,)), dma((doubles,)), dma((doubles,))]
        + [dma((3,))] * 4
        + [dma((5,))] * 2
        + [dma, dma],
        compiler_params=pltpu.CompilerParams(collective_id=0, has_side_effects=True),
    )(*streams, short_taps, residues, decay_rates)
    return pl.pallas_call(
        functools.partial(closing_kernel, own, taps),
        out_shape=[jax.ShapeDtypeStruct(queries.shape, BF16)] * 4
        + [jax.ShapeDtypeStruct(short_taps.shape, F32), mode_shape, mode_shape],
        in_specs=[here] * 7,
        out_specs=[here] * 7,
    )(*results)


def solution(mesh):
    stream = P("dp", None, "context")
    in_specs = (stream,) * 4 + (P(), P("context", None), P("context", None))
    out_specs = (stream,) * 4 + (P(), P("context", None), P("context", None))
    return jax.shard_map(per_device, mesh=mesh, in_specs=in_specs, out_specs=out_specs, check_vma=False)
```

```python
import functools
import math

import jax
import jax.numpy as jnp
from jax import lax
from jax.experimental import pallas as pl
from jax.experimental.pallas import tpu as pltpu
from jax.sharding import PartitionSpec as P

F32 = jnp.float32
BF16 = jnp.bfloat16
HIGHEST = lax.Precision.HIGHEST
LANES = 128
SUBS = 8
GROUP = 16
TALL = 8
WIDE = 4
PLANE = 8
PAIR = 2


def rounded(x):
    return x.astype(BF16).astype(F32)


MESH = pl.DeviceIdType.MESH


def place(index):
    return index // (TALL * WIDE), lax.rem(index // WIDE, TALL), lax.rem(index, WIDE)


def context_of(y, z, x):
    return (y * TALL + z) * WIDE + x


def settle(ref, send, recv=None):
    pltpu.make_async_copy(ref, ref, send).wait()
    if recv is not None:
        pltpu.make_async_copy(ref, ref, recv).wait()


def operator_kernel(
    modes, taps, steps, doubles, scale,
    q_ref, k_ref, v_ref, c_ref, taps_ref, residue_ref, rate_ref,
    out_ref, dq_ref, dk_ref, dv_ref, shared_ref, dres_ref, drate_ref,
    mq, mk, mv, mc, oo, oq, ok, ov,
    xq, xk, xv, xc, qs, ks, vs, gs, us, ys, ss, aq, ak, av,
    tab, logs, lst, pst, past, qacc, racc, tacc,
    tsrc, tin, fsrc, fin, bsrc, bin_, rims, tails,
    tap_part, tap_stack, first_part, first_stack, mode_part, mode_stack, mode_slots, total_ref,
    in_send, in_recv, out_send, out_recv, keep_sem, pair_send, pair_recv,
    rim_send, rim_recv, tail_send, tail_recv, line_send, line_recv, tap_send, tap_recv,
):
    y, z, x = place(lax.axis_index("context"))
    mine = lax.axis_index("dp")
    spot = y * WIDE + x
    own = residue_ref.shape[0]
    barrier = pltpu.get_barrier_semaphore()

    def across(step):
        s = lax.rem(spot + step, PLANE)
        return s, {"context": context_of(s // WIDE, z, lax.rem(s, WIDE))}

    def along(step):
        return {"context": context_of(y, lax.rem(z + step, TALL), x)}

    outer, inner = mine // PAIR, lax.rem(mine, PAIR)
    tower, field = z * PAIR + inner, spot * PAIR + outer

    def in_tower(step):
        q = lax.rem(tower + step, TALL * PAIR)
        return {"dp": outer * PAIR + lax.rem(q, PAIR), "context": context_of(y, q // PAIR, x)}

    def in_field(step):
        q = lax.rem(field + step, PLANE * PAIR)
        s = q // PAIR
        return {
            "dp": lax.rem(q, PAIR) * PAIR + inner,
            "context": context_of(s // WIDE, z, lax.rem(s, WIDE)),
        }

    for step in range(1, TALL * PAIR):
        pl.semaphore_signal(barrier, inc=1, device_id=in_tower(step), device_id_type=MESH)
    for step in range(1, PLANE * PAIR):
        pl.semaphore_signal(barrier, inc=1, device_id=in_field(step), device_id_type=MESH)
    pl.semaphore_signal(barrier, inc=1, device_id={"dp": doubles - 1 - mine}, device_id_type=MESH)

    sources, landed = (k_ref, v_ref, q_ref, c_ref), (mk, mv, mq, mc)
    kept = [
        pltpu.make_async_copy(sources[n].at[y, :, x], landed[n].at[spot], keep_sem.at[n]) for n in range(4)
    ]
    for copy in kept:
        copy.start()

    lane = lax.broadcasted_iota(jnp.int32, (SUBS, LANES), 1)
    sub = lax.broadcasted_iota(jnp.int32, (SUBS, LANES), 0)
    step_x = lax.rem(sub, WIDE)
    high = sub >= WIDE

    def at(t):
        return pl.ds(pl.multiple_of(t * SUBS, SUBS), SUBS)

    def fixed(row):
        return pl.ds(row * SUBS, SUBS)

    mine_lanes = (
        lax.broadcasted_iota(jnp.int32, (own, LANES), 1)
        == z * own + lax.broadcasted_iota(jnp.int32, (own, LANES), 0)
    ).astype(F32)
    turn = (((0,), (0,)), ((), ()))
    tsrc[pl.ds(0, modes), :] = lax.dot_general(
        residue_ref[...], mine_lanes, turn, precision=HIGHEST, preferred_element_type=F32
    )
    tsrc[pl.ds(modes, modes), :] = lax.dot_general(
        rate_ref[...], mine_lanes, turn, precision=HIGHEST, preferred_element_type=F32
    )
    half = taps_ref.shape[2] // 2
    column = lax.broadcasted_iota(jnp.int32, (half, LANES), 1)
    chosen = (
        lax.broadcasted_iota(jnp.int32, (half, LANES), 0)
        == column // own * (WIDE * own) + x * own + lax.rem(column, own)
    ).astype(F32)
    block = pl.ds(pl.multiple_of(y * half, half), half)
    n_taps = 2 * modes
    for stream in range(3):
        picked = jnp.dot(taps_ref[stream, :, block], chosen, precision=HIGHEST, preferred_element_type=F32)
        for j in range(taps):
            tab[fixed(n_taps + stream * taps + j), :] = jnp.broadcast_to(picked[j : j + 1, :], (SUBS, LANES))
    tacc[...] = jnp.zeros(tacc.shape, F32)

    def line(src, dst, n):
        for step in range(1, TALL):
            pltpu.make_async_remote_copy(
                src_ref=src,
                dst_ref=dst.at[z],
                send_sem=line_send.at[n],
                recv_sem=line_recv.at[n],
                device_id=along(step),
                device_id_type=MESH,
            ).start()
        copy = pltpu.make_async_copy(src, dst.at[z], keep_sem.at[8 + n])
        copy.start()
        return copy

    def line_wait(copy, dst, n):
        copy.wait()
        settle(dst.at[pl.ds(0, TALL - 1)], line_send.at[n], line_recv.at[n])

    pl.semaphore_wait(barrier, TALL * PAIR + PLANE * PAIR - 1)
    table_copy = line(tsrc, tin, 0)
    for n in range(4):
        for step in range(1, PLANE):
            s, peer = across(step)
            pltpu.make_async_remote_copy(
                src_ref=sources[n].at[s // WIDE, :, lax.rem(s, WIDE)],
                dst_ref=landed[n].at[spot],
                send_sem=in_send.at[n],
                recv_sem=in_recv.at[n],
                device_id=peer,
                device_id_type=MESH,
            ).start()

    line_wait(table_copy, tin, 0)
    tables = tin[0]
    for n in range(1, TALL):
        tables = tables + tin[n]
    residue, rate = tables[:modes], tables[modes:]
    double = 2.0 * rate
    series = 1.0 - double / 7.0
    for n in range(6, 1, -1):
        series = 1.0 - double / float(n) * series
    size = jnp.sqrt(double * series)
    damp = jnp.exp(-rate)
    weighted = residue * size
    for m in range(modes):
        tab[fixed(m), :] = jnp.broadcast_to(damp[m : m + 1, :], (SUBS, LANES))
        tab[fixed(modes + m), :] = jnp.broadcast_to(weighted[m : m + 1, :], (SUBS, LANES))
        logs[fixed(m), :] = jnp.broadcast_to(-float(steps) * rate[m : m + 1, :], (SUBS, LANES))

    def entry(row):
        return tab[fixed(row), :]

    ones = (
        lax.broadcasted_iota(jnp.int32, (LANES, LANES), 0)
        == lax.broadcasted_iota(jnp.int32, (LANES, LANES), 1)
    ).astype(BF16)

    def flipped(value):
        return lax.dot_general(ones, value, (((1,), (1,)), ((), ())), preferred_element_type=F32)

    reach = taps - 1
    head = reach * SUBS

    def unpack(n, dst):
        kept[n].wait()
        settle(landed[n].at[pl.ds(0, PLANE - 1)], in_recv.at[n])
        for i in range(PLANE):
            dst[pl.ds(head + i, steps, stride=SUBS), :] = flipped(landed[n][i].reshape(LANES, steps))

    def rim_copy(n, src):
        return pltpu.make_async_remote_copy(
            src_ref=src.at[pl.ds(steps * SUBS, head)],
            dst_ref=rims.at[n],
            send_sem=rim_send.at[n],
            recv_sem=rim_recv.at[n],
            device_id=along(1),
            device_id_type=MESH,
        )

    def tail_copy(n, src):
        return pltpu.make_async_remote_copy(
            src_ref=src.at[pl.ds(0, head)],
            dst_ref=tails.at[n],
            send_sem=tail_send.at[n],
            recv_sem=tail_recv.at[n],
            device_id=along(TALL - 1),
            device_id_type=MESH,
        )

    first_z, last_z = z == 0, z == TALL - 1

    def before(value, outer):
        lowest = jnp.where(high, pltpu.roll(outer, 1, 0), 0.0)
        outer = jnp.where(first_z, lowest, pltpu.roll(outer, 5, 0))
        return jnp.where(step_x > 0, pltpu.roll(value, 1, 0), outer)

    def after(value, outer):
        highest = jnp.where(high, 0.0, pltpu.roll(outer, 7, 0))
        outer = jnp.where(last_z, highest, pltpu.roll(outer, 3, 0))
        return jnp.where(step_x < WIDE - 1, pltpu.roll(value, 7, 0), outer)

    def rim(n, ref):
        for j in range(reach):
            ref[fixed(j), :] = before(ref[fixed(steps + j), :], rims[n, fixed(j), :])

    def tail(n, ref):
        for j in range(reach):
            ref[fixed(steps + j), :] = after(ref[fixed(j), :], tails[n, fixed(j), :])

    def tap(stream, j):
        return entry(n_taps + stream * taps + j)

    def filtered(ref, stream, t):
        total = tap(stream, 0) * ref[at(t + reach), :]
        for j in range(1, taps):
            total = total + tap(stream, j) * ref[at(t + reach - j), :]
        return rounded(total)

    def pair_features(t, carry):
        key, value = filtered(xk, 1, t), filtered(xv, 2, t)
        ks[at(t), :] = key
        vs[at(t), :] = value
        gs[at(t), :] = rounded(key * value)
        return carry

    def query_features(t, carry):
        query = filtered(xq, 0, t)
        qs[at(t), :] = query
        us[at(t), :] = rounded(xc[at(t + reach), :] * query)
        return carry

    zero = jnp.zeros((SUBS, LANES), F32)
    zeros = tuple(zero for _ in range(modes))

    def ahead_step(t, carry):
        gated = gs[at(t), :]
        return tuple(entry(m) * carry[m] + gated for m in range(modes))

    def back_step(i, carry):
        upstream = us[at(steps - 1 - i), :]
        return tuple(entry(m) * carry[m] + upstream for m in range(modes))

    def scan_ahead(value, m):
        power = jnp.exp(logs[fixed(m), :])
        for by in (1, 2):
            value = value + power * jnp.where(step_x >= by, pltpu.roll(value, by, 0), 0.0)
            power = power * power
        return value

    def scan_back(value, m):
        power = jnp.exp(logs[fixed(m), :])
        for by in (1, 2):
            value = value + power * jnp.where(step_x < WIDE - by, pltpu.roll(value, SUBS - by, 0), 0.0)
            power = power * power
        return value

    def ahead_row(n):
        return step_x == WIDE - 1 - n

    def back_row(n):
        return step_x == n

    def finish_ends(ends, scan, store, src, row_of, sign):
        for g in range(modes // WIDE):
            packed = zero
            for n in range(WIDE):
                m = g * WIDE + n
                value = scan(ends[m], m)
                store[fixed(m), :] = value
                packed = jnp.where(row_of(n), value if n == 0 else pltpu.roll(value, (sign * n) % SUBS, 0), packed)
            src[fixed(g), :] = packed

    def seeds(store, held, row_of, sign, order, inside, leap, fresh, weight):
        for g in range(modes // WIDE):
            slow = zero
            for n in range(WIDE):
                slow = jnp.where(row_of(n), logs[fixed(g * WIDE + n), :], slow)
            far = jnp.exp(float(WIDE) * slow)
            full, part = zero, zero
            for other in order:
                value = held[other, fixed(g), :]
                full = far * full + value
                part = jnp.where(inside(other), far * part + value, part)
            part = part + jnp.where(fresh, jnp.exp(slow * leap) * pltpu.roll(full, WIDE, 0), 0.0)
            for n in range(WIDE):
                m = g * WIDE + n
                value = jnp.where(row_of(n), part, 0.0)
                if n:
                    value = pltpu.roll(value, (-sign * n) % SUBS, 0)
                value = value + pltpu.roll(value, sign % SUBS, 0)
                value = value + pltpu.roll(value, (2 * sign) % SUBS, 0)
                value = jnp.exp(logs[fixed(m), :] * weight) * value
                near = pltpu.roll(store[fixed(m), :], (-sign) % SUBS, 0)
                keep = step_x > 0 if sign < 0 else step_x < WIDE - 1
                store[fixed(m), :] = jnp.where(keep, near, 0.0) + value

    float_x = step_x.astype(F32)
    float_z = z.astype(F32)

    unpack(0, xk)
    unpack(1, xv)
    rim_copies = [rim_copy(0, xk), rim_copy(1, xv)]
    for copy in rim_copies:
        copy.start()
    lax.fori_loop(reach, steps, pair_features, 0, unroll=6)
    ends = lax.fori_loop(reach, steps, ahead_step, zeros, unroll=6)
    for copy in rim_copies:
        copy.wait()
    rim(0, xk)
    rim(1, xv)
    for t in range(reach):
        pair_features(t, 0)
    ends = list(ends)
    for m in range(modes):
        for t in range(reach):
            ends[m] = ends[m] + jnp.exp(logs[fixed(m), :] * (float(steps - 1 - t) / steps)) * gs[fixed(t), :]
    finish_ends(ends, scan_ahead, lst, fsrc, ahead_row, -1)
    unpack(2, xq)
    ahead_copy = line(fsrc, fin, 1)
    query_rim = rim_copy(2, xq)
    query_rim.start()
    unpack(3, xc)
    query_rim.wait()
    rim(2, xq)
    lax.fori_loop(0, steps, query_features, 0, unroll=4)
    ends = lax.fori_loop(0, steps, back_step, zeros, unroll=4)
    finish_ends(ends, scan_back, pst, bsrc, back_row, 1)
    back_copy = line(bsrc, bin_, 2)
    line_wait(ahead_copy, fin, 1)
    seeds(
        lst, fin, ahead_row, -1, range(TALL), lambda other: other < z, float(WIDE) * float_z, high, float_x
    )

    for group in range(0, modes, GROUP):
        members = range(group, group + GROUP)

        def forward(t, carry):
            states, firsts = carry
            gated = gs[at(t), :]
            upstream = us[at(t), :]
            total = zero if group == 0 else ys[at(t), :]
            new_s, new_f = [], []
            for n, m in enumerate(members):
                past[at(t * modes + m), :] = states[n]
                state = entry(m) * states[n] + gated
                new_f.append(firsts[n] + upstream * state)
                total = total + entry(modes + m) * state
                new_s.append(state)
            ys[at(t), :] = total
            return tuple(new_s), tuple(new_f)

        few = tuple(zero for _ in members)
        _, firsts = lax.fori_loop(0, steps, forward, (tuple(lst[fixed(m), :] for m in members), few), unroll=4)
        for n, m in enumerate(members):
            qacc[pl.ds(m, 1), :] = jnp.sum(firsts[n], axis=0, keepdims=True)

    def gradient(a, stream, t):
        total = tap(stream, 0) * a[at(t), :]
        for j in range(1, taps):
            total = total + tap(stream, j) * a[at(t + j), :]
        return total

    def pack(src, dst):
        for i in range(PLANE):
            value = src[pl.ds(i, steps, stride=SUBS), :].astype(BF16)
            dst[i] = flipped(value).astype(BF16).reshape(dst.shape[1:])

    def query_products(t, carry):
        mixed = rounded(ys[at(t), :])
        ys[at(t), :] = qs[at(t), :] * mixed
        grad = rounded(xc[at(t + reach), :] * mixed)
        aq[at(t), :] = grad
        return tuple(carry[j] + grad * xq[at(t + reach - j), :] for j in range(taps))

    def query_gradients(t, carry):
        ss[at(t), :] = gradient(aq, 0, t)
        return carry

    results, outputs = (oo, oq, ok, ov), (out_ref, dq_ref, dk_ref, dv_ref)
    kept_out = []

    def deliver(n):
        for step in range(1, PLANE):
            s, peer = across(step)
            pltpu.make_async_remote_copy(
                src_ref=results[n].at[s],
                dst_ref=outputs[n].at[y, :, x],
                send_sem=out_send.at[n],
                recv_sem=out_recv.at[n],
                device_id=peer,
                device_id_type=MESH,
            ).start()
        copy = pltpu.make_async_copy(results[n].at[spot], outputs[n].at[y, :, x], keep_sem.at[4 + n])
        copy.start()
        kept_out.append(copy)

    first_part[...] = scale * size * qacc[...]
    sums = lax.fori_loop(0, steps, query_products, tuple(zero for _ in range(taps)), unroll=4)
    for n in range(taps):
        tacc[pl.ds(n, 1), :] = jnp.sum(sums[n], axis=0, keepdims=True)
    query_tail = tail_copy(0, aq)
    query_tail.start()
    first_copy = line(first_part, first_stack, 5)
    pack(ys, oo)
    query_tail.wait()
    tail(0, aq)
    deliver(0)
    lax.fori_loop(0, steps, query_gradients, 0, unroll=4)
    pack(ss, oq)
    line_wait(back_copy, bin_, 2)
    seeds(
        pst, bin_, back_row, 1, range(TALL - 1, -1, -1), lambda other: other > z,
        float(WIDE) * (float(TALL - 1) - float_z), jnp.logical_not(high), float(WIDE - 1) - float_x,
    )
    deliver(1)

    for group in range(0, modes, GROUP):
        members = range(group, group + GROUP)

        def backward(i, carry):
            states, seconds = carry
            t = steps - 1 - i
            upstream = us[at(t), :]
            total = zero if group == 0 else ss[at(t), :]
            new_s, new_r = [], []
            for n, m in enumerate(members):
                state = entry(m) * states[n] + upstream
                new_r.append(seconds[n] + state * past[at(t * modes + m), :])
                total = total + entry(modes + m) * state
                new_s.append(state)
            ss[at(t), :] = total
            return tuple(new_s), tuple(new_r)

        few = tuple(zero for _ in members)
        _, seconds = lax.fori_loop(0, steps, backward, (tuple(pst[fixed(m), :] for m in members), few), unroll=4)
        for n, m in enumerate(members):
            racc[pl.ds(m, 1), :] = jnp.sum(seconds[n], axis=0, keepdims=True)

    def pair_products(t, carry):
        source = rounded(ss[at(t), :])
        new = []
        for n, (other, ref, x_ref) in enumerate(((vs, ak, xk), (ks, av, xv))):
            grad = rounded(source * other[at(t), :])
            ref[at(t), :] = grad
            for j in range(taps):
                new.append(carry[n * taps + j] + grad * x_ref[at(t + reach - j), :])
        return tuple(new)

    def key_gradients(t, carry):
        ys[at(t), :] = gradient(ak, 1, t)
        return carry

    def value_gradients(t, carry):
        ss[at(t), :] = gradient(av, 2, t)
        return carry

    sums = lax.fori_loop(0, steps, pair_products, tuple(zero for _ in range(2 * taps)), unroll=4)
    for n in range(2 * taps):
        tacc[pl.ds(taps + n, 1), :] = jnp.sum(sums[n], axis=0, keepdims=True)
    tail_copies = [tail_copy(1, ak), tail_copy(2, av)]
    for copy in tail_copies:
        copy.start()
    tap_part[...] = scale * tacc[...]
    first, second = qacc[...], racc[...] * damp
    mode_part[...] = scale * rate * (residue * (damp * damp / size) * first - weighted * second)
    for step in range(1, TALL * PAIR):
        pltpu.make_async_remote_copy(
            src_ref=tap_part,
            dst_ref=tap_stack.at[tower],
            send_sem=line_send.at[3],
            recv_sem=line_recv.at[3],
            device_id=in_tower(step),
            device_id_type=MESH,
        ).start()
    tap_copy = pltpu.make_async_copy(tap_part, tap_stack.at[tower], keep_sem.at[11])
    tap_copy.start()
    mode_copy = line(mode_part, mode_stack, 4)
    lax.fori_loop(0, steps - reach, key_gradients, 0, unroll=6)
    for copy in tail_copies:
        copy.wait()
    tail(1, ak)
    tail(2, av)
    for t in range(steps - reach, steps):
        key_gradients(t, 0)
    pack(ys, ok)
    lax.fori_loop(0, steps // 4, value_gradients, 0, unroll=8)
    deliver(2)
    lax.fori_loop(steps // 4, steps, value_gradients, 0, unroll=8)
    pack(ss, ov)
    deliver(3)

    def summed(ref, count):
        total = ref[0]
        for n in range(1, count):
            total = total + ref[n]
        return total

    line_wait(first_copy, first_stack, 5)
    mode_slots[doubles, pl.ds(0, modes), :] = summed(first_stack, TALL)
    tap_copy.wait()
    settle(tap_stack.at[pl.ds(0, TALL * PAIR - 1)], line_send.at[3], line_recv.at[3])
    total_ref[...] = summed(tap_stack, TALL * PAIR)
    for step in range(1, PLANE * PAIR):
        pltpu.make_async_remote_copy(
            src_ref=total_ref,
            dst_ref=shared_ref.at[field],
            send_sem=tap_send,
            recv_sem=tap_recv,
            device_id=in_field(step),
            device_id_type=MESH,
        ).start()
    own_taps = pltpu.make_async_copy(total_ref, shared_ref.at[field], keep_sem.at[15])
    own_taps.start()
    line_wait(mode_copy, mode_stack, 4)
    mode_slots[doubles, pl.ds(modes, modes), :] = summed(mode_stack, TALL)
    mode_pairs = [
        pltpu.make_async_remote_copy(
            src_ref=mode_slots.at[doubles],
            dst_ref=mode_slots.at[mine],
            send_sem=pair_send.at[step],
            recv_sem=pair_recv.at[step],
            device_id={"dp": lax.rem(mine + step, doubles)},
            device_id_type=MESH,
        )
        for step in range(1, doubles)
    ]
    mode_pairs.append(pltpu.make_async_copy(mode_slots.at[doubles], mode_slots.at[mine], keep_sem.at[14]))
    for pair in mode_pairs:
        pair.start()
    for pair in mode_pairs:
        pair.wait()
    total = summed(mode_slots, doubles)
    for ref, start in ((dres_ref, 0), (drate_ref, modes)):
        ref[...] = lax.dot_general(
            mine_lanes,
            total[start : start + modes],
            (((1,), (1,)), ((), ())),
            precision=HIGHEST,
            preferred_element_type=F32,
        )
    for n in range(4):
        settle(landed[n].at[pl.ds(0, PLANE - 1)], in_send.at[n])
    for copy in kept_out:
        copy.wait()
    own_taps.wait()
    for n in range(4):
        settle(results[n].at[pl.ds(0, PLANE - 1)], out_send.at[n])
        settle(outputs[n].at[:, pl.ds(0, TALL - 1)], out_recv.at[n])
    settle(shared_ref.at[pl.ds(0, PLANE * PAIR - 1)], tap_send, tap_recv)


def closing_kernel(own, taps, *refs):
    sources, shared_ref, parts, targets = refs[:4], refs[4], refs[5:7], refs[7:11]
    taps_ref, finals = refs[11], refs[12:]
    for source, target in zip(sources, targets):
        target[0] = source[...].reshape(target.shape[1:])
    for part, final in zip(parts, finals):
        final[...] = part[...]
    rows = shared_ref.shape[1]
    group = lax.broadcasted_iota(jnp.int32, (rows, LANES), 1) // own
    groups = LANES // own
    for b in range(taps_ref.shape[2] // LANES):
        y, pair = b // WIDE, b % WIDE
        value = jnp.zeros((rows, LANES), F32)
        for spot in range(groups):
            z, x = pair * (groups // WIDE) + spot // WIDE, spot % WIDE
            first = (y * WIDE + x) * PAIR
            held = shared_ref[first] + shared_ref[first + 1]
            held = pltpu.roll(held, (spot - z) * own % LANES, 1)
            value = jnp.where(group == spot, held, value)
        for stream in range(3):
            taps_ref[stream, :, pl.ds(b * LANES, LANES)] = value[stream * taps : (stream + 1) * taps]


def per_device(queries, key_stream, value_stream, cotangent, short_taps, residues, decay_rates):
    channels, steps = queries.shape[1], queries.shape[2]
    own, modes = residues.shape
    taps = short_taps.shape[1]
    owners, doubles = lax.axis_size("context"), lax.axis_size("dp")
    scale = 1.0 / math.sqrt(queries.shape[0] * doubles * steps * owners)
    view = (owners // (TALL * WIDE), TALL, WIDE, own, steps)
    wide = jax.ShapeDtypeStruct(view, BF16)
    mode_shape = jax.ShapeDtypeStruct(residues.shape, F32)
    line, reach = steps * SUBS, taps - 1
    vm = pltpu.VMEM
    here = pl.BlockSpec(memory_space=vm)
    away = pl.BlockSpec(memory_space=pl.ANY)
    dma = pltpu.SemaphoreType.DMA
    tap_rows = 3 * taps
    ends = modes // WIDE * SUBS
    streams = [x.reshape(view) for x in (queries, key_stream, value_stream, cotangent)]
    results = pl.pallas_call(
        functools.partial(operator_kernel, modes, taps, steps, doubles, scale),
        out_shape=[vm(view, BF16)] * 4 + [vm((PLANE * PAIR, tap_rows, LANES), F32), vm(residues.shape, F32), vm(residues.shape, F32)],
        in_specs=[away] * 4 + [here] * 3,
        out_specs=[here] * 7,
        scratch_shapes=[vm((PLANE, TALL, own, steps), BF16)] * 8
        + [vm((line + reach * SUBS, LANES), F32)] * 4
        + [vm((line, LANES), F32)] * 7
        + [vm((line + reach * SUBS, LANES), F32)] * 3
        + [
            vm(((2 * modes + 3 * taps) * SUBS, LANES), F32),
            vm((modes * SUBS, LANES), F32),
            vm((modes * SUBS, LANES), F32),
            vm((modes * SUBS, LANES), F32),
            vm((line * modes, LANES), F32),
            vm((modes, LANES), F32),
            vm((modes, LANES), F32),
            vm((tap_rows, LANES), F32),
            vm((2 * modes, LANES), F32),
            vm((TALL, 2 * modes, LANES), F32),
            vm((ends, LANES), F32),
            vm((TALL, ends, LANES), F32),
            vm((ends, LANES), F32),
            vm((TALL, ends, LANES), F32),
            vm((3, reach * SUBS, LANES), F32),
            vm((3, reach * SUBS, LANES), F32),
            vm((tap_rows, LANES), F32),
            vm((TALL * PAIR, tap_rows, LANES), F32),
            vm((modes, LANES), F32),
            vm((TALL, modes, LANES), F32),
            vm((modes, LANES), F32),
            vm((TALL, modes, LANES), F32),
            vm((doubles + 1, 2 * modes, LANES), F32),
            vm((tap_rows, LANES), F32),
        ]
        + [dma((4,))] * 4
        + [dma((16,)), dma((doubles,)), dma((doubles,))]
        + [dma((3,))] * 4
        + [dma((6,))] * 2
        + [dma, dma],
        compiler_params=pltpu.CompilerParams(collective_id=0, has_side_effects=True, vmem_limit_bytes=58 * 1024 * 1024),
    )(*streams, short_taps, residues, decay_rates)
    return pl.pallas_call(
        functools.partial(closing_kernel, own, taps),
        out_shape=[jax.ShapeDtypeStruct(queries.shape, BF16)] * 4
        + [jax.ShapeDtypeStruct(short_taps.shape, F32), mode_shape, mode_shape],
        in_specs=[here] * 7,
        out_specs=[here] * 7,
        compiler_params=pltpu.CompilerParams(vmem_limit_bytes=16 * 1024 * 1024),
    )(*results)


def solution(mesh):
    stream = P("dp", None, "context")
    in_specs = (stream,) * 4 + (P(), P("context", None), P("context", None))
    out_specs = (stream,) * 4 + (P(), P("context", None), P("context", None))
    return jax.shard_map(per_device, mesh=mesh, in_specs=in_specs, out_specs=out_specs, check_vma=False)
```

```python
import functools
import math

import jax
import jax.numpy as jnp
from jax import lax
from jax.experimental import pallas as pl
from jax.experimental.pallas import tpu as pltpu
from jax.sharding import PartitionSpec as P

F32 = jnp.float32
BF16 = jnp.bfloat16
HIGHEST = lax.Precision.HIGHEST
LANES = 128
SUBS = 8
GROUP = 16
TALL = 8
WIDE = 4
PLANE = 8
PAIR = 2


def rounded(x):
    return x.astype(BF16).astype(F32)


MESH = pl.DeviceIdType.MESH


def place(index):
    return index // (TALL * WIDE), lax.rem(index // WIDE, TALL), lax.rem(index, WIDE)


def context_of(y, z, x):
    return (y * TALL + z) * WIDE + x


def settle(ref, send, recv=None):
    pltpu.make_async_copy(ref, ref, send).wait()
    if recv is not None:
        pltpu.make_async_copy(ref, ref, recv).wait()


def operator_kernel(
    modes, taps, steps, doubles, scale,
    q_ref, k_ref, v_ref, c_ref, taps_ref, residue_ref, rate_ref,
    out_ref, dq_ref, dk_ref, dv_ref, shared_ref, dres_ref, drate_ref,
    mq, mk, mv, mc, oo, oq, ok, ov,
    xq, xk, xv, xc, qs, ks, vs, gs, us, ys, ss, aq, ak, av,
    tab, logs, lst, pst, past, qacc, racc, tacc,
    tsrc, tin, fsrc, fin, bsrc, bin_, rims, tails,
    tap_part, tap_stack, first_part, first_stack, mode_part, mode_stack, mode_slots, total_ref,
    in_send, in_recv, out_send, out_recv, keep_sem, pair_send, pair_recv,
    rim_send, rim_recv, tail_send, tail_recv, line_send, line_recv, tap_send, tap_recv,
):
    y, z, x = place(lax.axis_index("context"))
    mine = lax.axis_index("dp")
    spot = y * WIDE + x
    own = residue_ref.shape[0]
    barrier = pltpu.get_barrier_semaphore()

    def across(step):
        s = lax.rem(spot + step, PLANE)
        return s, {"context": context_of(s // WIDE, z, lax.rem(s, WIDE))}

    def along(step):
        return {"context": context_of(y, lax.rem(z + step, TALL), x)}

    outer, inner = mine // PAIR, lax.rem(mine, PAIR)
    tower, field = z * PAIR + inner, spot * PAIR + outer

    def in_tower(step):
        q = lax.rem(tower + step, TALL * PAIR)
        return {"dp": outer * PAIR + lax.rem(q, PAIR), "context": context_of(y, q // PAIR, x)}

    def in_field(step):
        q = lax.rem(field + step, PLANE * PAIR)
        s = q // PAIR
        return {
            "dp": lax.rem(q, PAIR) * PAIR + inner,
            "context": context_of(s // WIDE, z, lax.rem(s, WIDE)),
        }

    for step in range(1, TALL * PAIR):
        pl.semaphore_signal(barrier, inc=1, device_id=in_tower(step), device_id_type=MESH)
    for step in range(1, PLANE * PAIR):
        pl.semaphore_signal(barrier, inc=1, device_id=in_field(step), device_id_type=MESH)
    pl.semaphore_signal(barrier, inc=1, device_id={"dp": doubles - 1 - mine}, device_id_type=MESH)

    sources, landed = (k_ref, v_ref, q_ref, c_ref), (mk, mv, mq, mc)
    kept = [
        pltpu.make_async_copy(sources[n].at[y, :, x], landed[n].at[spot], keep_sem.at[n]) for n in range(4)
    ]
    for copy in kept:
        copy.start()

    lane = lax.broadcasted_iota(jnp.int32, (SUBS, LANES), 1)
    sub = lax.broadcasted_iota(jnp.int32, (SUBS, LANES), 0)
    step_x = lax.rem(sub, WIDE)
    high = sub >= WIDE

    def at(t):
        return pl.ds(pl.multiple_of(t * SUBS, SUBS), SUBS)

    def fixed(row):
        return pl.ds(row * SUBS, SUBS)

    mine_lanes = (
        lax.broadcasted_iota(jnp.int32, (own, LANES), 1)
        == z * own + lax.broadcasted_iota(jnp.int32, (own, LANES), 0)
    ).astype(F32)
    turn = (((0,), (0,)), ((), ()))
    tsrc[pl.ds(0, modes), :] = lax.dot_general(
        residue_ref[...], mine_lanes, turn, precision=HIGHEST, preferred_element_type=F32
    )
    tsrc[pl.ds(modes, modes), :] = lax.dot_general(
        rate_ref[...], mine_lanes, turn, precision=HIGHEST, preferred_element_type=F32
    )
    half = taps_ref.shape[2] // 2
    column = lax.broadcasted_iota(jnp.int32, (half, LANES), 1)
    chosen = (
        lax.broadcasted_iota(jnp.int32, (half, LANES), 0)
        == column // own * (WIDE * own) + x * own + lax.rem(column, own)
    ).astype(F32)
    block = pl.ds(pl.multiple_of(y * half, half), half)
    n_taps = 2 * modes
    for stream in range(3):
        picked = jnp.dot(taps_ref[stream, :, block], chosen, precision=HIGHEST, preferred_element_type=F32)
        for j in range(taps):
            tab[fixed(n_taps + stream * taps + j), :] = jnp.broadcast_to(picked[j : j + 1, :], (SUBS, LANES))
    tacc[...] = jnp.zeros(tacc.shape, F32)

    def line(src, dst, n):
        for step in range(1, TALL):
            pltpu.make_async_remote_copy(
                src_ref=src,
                dst_ref=dst.at[z],
                send_sem=line_send.at[n],
                recv_sem=line_recv.at[n],
                device_id=along(step),
                device_id_type=MESH,
            ).start()
        copy = pltpu.make_async_copy(src, dst.at[z], keep_sem.at[8 + n])
        copy.start()
        return copy

    def line_wait(copy, dst, n):
        copy.wait()
        settle(dst.at[pl.ds(0, TALL - 1)], line_send.at[n], line_recv.at[n])

    pl.semaphore_wait(barrier, TALL * PAIR + PLANE * PAIR - 1)
    table_copy = line(tsrc, tin, 0)
    for n in range(4):
        for step in range(1, PLANE):
            s, peer = across(step)
            pltpu.make_async_remote_copy(
                src_ref=sources[n].at[s // WIDE, :, lax.rem(s, WIDE)],
                dst_ref=landed[n].at[spot],
                send_sem=in_send.at[n],
                recv_sem=in_recv.at[n],
                device_id=peer,
                device_id_type=MESH,
            ).start()

    line_wait(table_copy, tin, 0)
    tables = tin[0]
    for n in range(1, TALL):
        tables = tables + tin[n]
    residue, rate = tables[:modes], tables[modes:]
    double = 2.0 * rate
    series = 1.0 - double / 7.0
    for n in range(6, 1, -1):
        series = 1.0 - double / float(n) * series
    size = jnp.sqrt(double * series)
    damp = jnp.exp(-rate)
    weighted = residue * size
    for m in range(modes):
        tab[fixed(m), :] = jnp.broadcast_to(damp[m : m + 1, :], (SUBS, LANES))
        tab[fixed(modes + m), :] = jnp.broadcast_to(weighted[m : m + 1, :], (SUBS, LANES))
        logs[fixed(m), :] = jnp.broadcast_to(-float(steps) * rate[m : m + 1, :], (SUBS, LANES))

    def entry(row):
        return tab[fixed(row), :]

    ones = (
        lax.broadcasted_iota(jnp.int32, (LANES, LANES), 0)
        == lax.broadcasted_iota(jnp.int32, (LANES, LANES), 1)
    ).astype(BF16)

    def flipped(value):
        return lax.dot_general(ones, value, (((1,), (1,)), ((), ())), preferred_element_type=F32)

    reach = taps - 1
    head = reach * SUBS

    def unpack(n, dst):
        kept[n].wait()
        settle(landed[n].at[pl.ds(0, PLANE - 1)], in_recv.at[n])
        for i in range(PLANE):
            dst[pl.ds(head + i, steps, stride=SUBS), :] = flipped(landed[n][i].reshape(LANES, steps))

    def rim_copy(n, src):
        return pltpu.make_async_remote_copy(
            src_ref=src.at[pl.ds(steps * SUBS, head)],
            dst_ref=rims.at[n],
            send_sem=rim_send.at[n],
            recv_sem=rim_recv.at[n],
            device_id=along(1),
            device_id_type=MESH,
        )

    def tail_copy(n, src):
        return pltpu.make_async_remote_copy(
            src_ref=src.at[pl.ds(0, head)],
            dst_ref=tails.at[n],
            send_sem=tail_send.at[n],
            recv_sem=tail_recv.at[n],
            device_id=along(TALL - 1),
            device_id_type=MESH,
        )

    first_z, last_z = z == 0, z == TALL - 1

    def before(value, outer):
        lowest = jnp.where(high, pltpu.roll(outer, 1, 0), 0.0)
        outer = jnp.where(first_z, lowest, pltpu.roll(outer, 5, 0))
        return jnp.where(step_x > 0, pltpu.roll(value, 1, 0), outer)

    def after(value, outer):
        highest = jnp.where(high, 0.0, pltpu.roll(outer, 7, 0))
        outer = jnp.where(last_z, highest, pltpu.roll(outer, 3, 0))
        return jnp.where(step_x < WIDE - 1, pltpu.roll(value, 7, 0), outer)

    def rim(n, ref):
        for j in range(reach):
            ref[fixed(j), :] = before(ref[fixed(steps + j), :], rims[n, fixed(j), :])

    def tail(n, ref):
        for j in range(reach):
            ref[fixed(steps + j), :] = after(ref[fixed(j), :], tails[n, fixed(j), :])

    def tap(stream, j):
        return entry(n_taps + stream * taps + j)

    def filtered(ref, stream, t):
        total = tap(stream, 0) * ref[at(t + reach), :]
        for j in range(1, taps):
            total = total + tap(stream, j) * ref[at(t + reach - j), :]
        return rounded(total)

    def pair_features(t, carry):
        key, value = filtered(xk, 1, t), filtered(xv, 2, t)
        ks[at(t), :] = key
        vs[at(t), :] = value
        gs[at(t), :] = rounded(key * value)
        return carry

    def query_features(t, carry):
        query = filtered(xq, 0, t)
        qs[at(t), :] = query
        us[at(t), :] = rounded(xc[at(t + reach), :] * query)
        return carry

    zero = jnp.zeros((SUBS, LANES), F32)
    zeros = tuple(zero for _ in range(modes))

    def ahead_step(t, carry):
        gated = gs[at(t), :]
        return tuple(entry(m) * carry[m] + gated for m in range(modes))

    def back_step(i, carry):
        upstream = us[at(steps - 1 - i), :]
        return tuple(entry(m) * carry[m] + upstream for m in range(modes))

    def scan_ahead(value, m):
        power = jnp.exp(logs[fixed(m), :])
        for by in (1, 2):
            value = value + power * jnp.where(step_x >= by, pltpu.roll(value, by, 0), 0.0)
            power = power * power
        return value

    def scan_back(value, m):
        power = jnp.exp(logs[fixed(m), :])
        for by in (1, 2):
            value = value + power * jnp.where(step_x < WIDE - by, pltpu.roll(value, SUBS - by, 0), 0.0)
            power = power * power
        return value

    def ahead_row(n):
        return step_x == WIDE - 1 - n

    def back_row(n):
        return step_x == n

    def finish_ends(ends, scan, store, src, row_of, sign):
        for g in range(modes // WIDE):
            packed = zero
            for n in range(WIDE):
                m = g * WIDE + n
                value = scan(ends[m], m)
                store[fixed(m), :] = value
                packed = jnp.where(row_of(n), value if n == 0 else pltpu.roll(value, (sign * n) % SUBS, 0), packed)
            src[fixed(g), :] = packed

    def seeds(store, held, row_of, sign, order, inside, leap, fresh, weight):
        for g in range(modes // WIDE):
            slow = zero
            for n in range(WIDE):
                slow = jnp.where(row_of(n), logs[fixed(g * WIDE + n), :], slow)
            far = jnp.exp(float(WIDE) * slow)
            full, part = zero, zero
            for other in order:
                value = held[other, fixed(g), :]
                full = far * full + value
                part = jnp.where(inside(other), far * part + value, part)
            part = part + jnp.where(fresh, jnp.exp(slow * leap) * pltpu.roll(full, WIDE, 0), 0.0)
            for n in range(WIDE):
                m = g * WIDE + n
                value = jnp.where(row_of(n), part, 0.0)
                if n:
                    value = pltpu.roll(value, (-sign * n) % SUBS, 0)
                value = value + pltpu.roll(value, sign % SUBS, 0)
                value = value + pltpu.roll(value, (2 * sign) % SUBS, 0)
                value = jnp.exp(logs[fixed(m), :] * weight) * value
                near = pltpu.roll(store[fixed(m), :], (-sign) % SUBS, 0)
                keep = step_x > 0 if sign < 0 else step_x < WIDE - 1
                store[fixed(m), :] = jnp.where(keep, near, 0.0) + value

    float_x = step_x.astype(F32)
    float_z = z.astype(F32)

    unpack(0, xk)
    unpack(1, xv)
    rim_copies = [rim_copy(0, xk), rim_copy(1, xv)]
    for copy in rim_copies:
        copy.start()
    lax.fori_loop(reach, steps, pair_features, 0, unroll=6)
    ends = lax.fori_loop(reach, steps, ahead_step, zeros, unroll=6)
    for copy in rim_copies:
        copy.wait()
    rim(0, xk)
    rim(1, xv)
    for t in range(reach):
        pair_features(t, 0)
    ends = list(ends)
    for m in range(modes):
        for t in range(reach):
            ends[m] = ends[m] + jnp.exp(logs[fixed(m), :] * (float(steps - 1 - t) / steps)) * gs[fixed(t), :]
    finish_ends(ends, scan_ahead, lst, fsrc, ahead_row, -1)
    unpack(2, xq)
    ahead_copy = line(fsrc, fin, 1)
    query_rim = rim_copy(2, xq)
    query_rim.start()
    unpack(3, xc)
    query_rim.wait()
    rim(2, xq)
    lax.fori_loop(0, steps, query_features, 0, unroll=4)
    ends = lax.fori_loop(0, steps, back_step, zeros, unroll=4)
    finish_ends(ends, scan_back, pst, bsrc, back_row, 1)
    back_copy = line(bsrc, bin_, 2)
    line_wait(ahead_copy, fin, 1)
    seeds(
        lst, fin, ahead_row, -1, range(TALL), lambda other: other < z, float(WIDE) * float_z, high, float_x
    )

    for group in range(0, modes, GROUP):
        members = range(group, group + GROUP)

        def forward(t, carry):
            states, firsts = carry
            gated = gs[at(t), :]
            upstream = us[at(t), :]
            total = zero if group == 0 else ys[at(t), :]
            new_s, new_f = [], []
            for n, m in enumerate(members):
                past[at(t * modes + m), :] = states[n]
                state = entry(m) * states[n] + gated
                new_f.append(firsts[n] + upstream * state)
                total = total + entry(modes + m) * state
                new_s.append(state)
            ys[at(t), :] = total
            return tuple(new_s), tuple(new_f)

        few = tuple(zero for _ in members)
        _, firsts = lax.fori_loop(0, steps, forward, (tuple(lst[fixed(m), :] for m in members), few), unroll=4)
        for n, m in enumerate(members):
            qacc[pl.ds(m, 1), :] = jnp.sum(firsts[n], axis=0, keepdims=True)

    def gradient(a, stream, t):
        total = tap(stream, 0) * a[at(t), :]
        for j in range(1, taps):
            total = total + tap(stream, j) * a[at(t + j), :]
        return total

    def pack(src, dst):
        for i in range(PLANE):
            value = src[pl.ds(i, steps, stride=SUBS), :].astype(BF16)
            dst[i] = flipped(value).astype(BF16).reshape(dst.shape[1:])

    def query_products(t, carry):
        mixed = rounded(ys[at(t), :])
        ys[at(t), :] = qs[at(t), :] * mixed
        grad = rounded(xc[at(t + reach), :] * mixed)
        aq[at(t), :] = grad
        return tuple(carry[j] + grad * xq[at(t + reach - j), :] for j in range(taps))

    def query_gradients(t, carry):
        ss[at(t), :] = gradient(aq, 0, t)
        return carry

    results, outputs = (oo, oq, ok, ov), (out_ref, dq_ref, dk_ref, dv_ref)
    kept_out = []

    def deliver(n):
        for step in range(1, PLANE):
            s, peer = across(step)
            pltpu.make_async_remote_copy(
                src_ref=results[n].at[s],
                dst_ref=outputs[n].at[y, :, x],
                send_sem=out_send.at[n],
                recv_sem=out_recv.at[n],
                device_id=peer,
                device_id_type=MESH,
            ).start()
        copy = pltpu.make_async_copy(results[n].at[spot], outputs[n].at[y, :, x], keep_sem.at[4 + n])
        copy.start()
        kept_out.append(copy)

    first_part[...] = scale * size * qacc[...]
    sums = lax.fori_loop(0, steps, query_products, tuple(zero for _ in range(taps)), unroll=4)
    for n in range(taps):
        tacc[pl.ds(n, 1), :] = jnp.sum(sums[n], axis=0, keepdims=True)
    query_tail = tail_copy(0, aq)
    query_tail.start()
    first_copy = line(first_part, first_stack, 5)
    pack(ys, oo)
    query_tail.wait()
    tail(0, aq)
    deliver(0)
    lax.fori_loop(0, steps, query_gradients, 0, unroll=4)
    pack(ss, oq)
    line_wait(back_copy, bin_, 2)
    seeds(
        pst, bin_, back_row, 1, range(TALL - 1, -1, -1), lambda other: other > z,
        float(WIDE) * (float(TALL - 1) - float_z), jnp.logical_not(high), float(WIDE - 1) - float_x,
    )
    deliver(1)

    for group in range(0, modes, GROUP):
        members = range(group, group + GROUP)

        def backward(i, carry):
            states, seconds = carry
            t = steps - 1 - i
            upstream = us[at(t), :]
            total = zero if group == 0 else ss[at(t), :]
            new_s, new_r = [], []
            for n, m in enumerate(members):
                state = entry(m) * states[n] + upstream
                new_r.append(seconds[n] + state * past[at(t * modes + m), :])
                total = total + entry(modes + m) * state
                new_s.append(state)
            ss[at(t), :] = total
            return tuple(new_s), tuple(new_r)

        few = tuple(zero for _ in members)
        _, seconds = lax.fori_loop(0, steps, backward, (tuple(pst[fixed(m), :] for m in members), few), unroll=4)
        for n, m in enumerate(members):
            racc[pl.ds(m, 1), :] = jnp.sum(seconds[n], axis=0, keepdims=True)

    def pair_products(t, carry):
        source = rounded(ss[at(t), :])
        new = []
        for n, (other, ref, x_ref) in enumerate(((vs, ak, xk), (ks, av, xv))):
            grad = rounded(source * other[at(t), :])
            ref[at(t), :] = grad
            for j in range(taps):
                new.append(carry[n * taps + j] + grad * x_ref[at(t + reach - j), :])
        return tuple(new)

    def key_gradients(t, carry):
        ys[at(t), :] = gradient(ak, 1, t)
        return carry

    def value_gradients(t, carry):
        ss[at(t), :] = gradient(av, 2, t)
        return carry

    sums = lax.fori_loop(0, steps, pair_products, tuple(zero for _ in range(2 * taps)), unroll=4)
    for n in range(2 * taps):
        tacc[pl.ds(taps + n, 1), :] = jnp.sum(sums[n], axis=0, keepdims=True)
    tail_copies = [tail_copy(1, ak), tail_copy(2, av)]
    for copy in tail_copies:
        copy.start()
    tap_part[...] = scale * tacc[...]
    first, second = qacc[...], racc[...] * damp
    mode_part[...] = scale * rate * (residue * (damp * damp / size) * first - weighted * second)
    for step in range(1, TALL * PAIR):
        pltpu.make_async_remote_copy(
            src_ref=tap_part,
            dst_ref=tap_stack.at[tower],
            send_sem=line_send.at[3],
            recv_sem=line_recv.at[3],
            device_id=in_tower(step),
            device_id_type=MESH,
        ).start()
    tap_copy = pltpu.make_async_copy(tap_part, tap_stack.at[tower], keep_sem.at[11])
    tap_copy.start()
    mode_copy = line(mode_part, mode_stack, 4)
    lax.fori_loop(0, steps - reach, key_gradients, 0, unroll=6)
    lax.fori_loop(0, steps - reach, value_gradients, 0, unroll=6)
    for copy in tail_copies:
        copy.wait()
    tail(1, ak)
    tail(2, av)
    for t in range(steps - reach, steps):
        key_gradients(t, 0)
    pack(ys, ok)
    for t in range(steps - reach, steps):
        value_gradients(t, 0)
    deliver(2)
    pack(ss, ov)
    deliver(3)

    def summed(ref, count):
        total = ref[0]
        for n in range(1, count):
            total = total + ref[n]
        return total

    line_wait(first_copy, first_stack, 5)
    mode_slots[doubles, pl.ds(0, modes), :] = summed(first_stack, TALL)
    tap_copy.wait()
    settle(tap_stack.at[pl.ds(0, TALL * PAIR - 1)], line_send.at[3], line_recv.at[3])
    total_ref[...] = summed(tap_stack, TALL * PAIR)
    for step in range(1, PLANE * PAIR):
        pltpu.make_async_remote_copy(
            src_ref=total_ref,
            dst_ref=shared_ref.at[field],
            send_sem=tap_send,
            recv_sem=tap_recv,
            device_id=in_field(step),
            device_id_type=MESH,
        ).start()
    own_taps = pltpu.make_async_copy(total_ref, shared_ref.at[field], keep_sem.at[15])
    own_taps.start()
    line_wait(mode_copy, mode_stack, 4)
    mode_slots[doubles, pl.ds(modes, modes), :] = summed(mode_stack, TALL)
    mode_pairs = [
        pltpu.make_async_remote_copy(
            src_ref=mode_slots.at[doubles],
            dst_ref=mode_slots.at[mine],
            send_sem=pair_send.at[step],
            recv_sem=pair_recv.at[step],
            device_id={"dp": lax.rem(mine + step, doubles)},
            device_id_type=MESH,
        )
        for step in range(1, doubles)
    ]
    mode_pairs.append(pltpu.make_async_copy(mode_slots.at[doubles], mode_slots.at[mine], keep_sem.at[14]))
    for pair in mode_pairs:
        pair.start()
    for pair in mode_pairs:
        pair.wait()
    total = summed(mode_slots, doubles)
    for ref, start in ((dres_ref, 0), (drate_ref, modes)):
        ref[...] = lax.dot_general(
            mine_lanes,
            total[start : start + modes],
            (((1,), (1,)), ((), ())),
            precision=HIGHEST,
            preferred_element_type=F32,
        )
    for n in range(4):
        settle(landed[n].at[pl.ds(0, PLANE - 1)], in_send.at[n])
    for copy in kept_out:
        copy.wait()
    own_taps.wait()
    for n in range(4):
        settle(results[n].at[pl.ds(0, PLANE - 1)], out_send.at[n])
        settle(outputs[n].at[:, pl.ds(0, TALL - 1)], out_recv.at[n])
    settle(shared_ref.at[pl.ds(0, PLANE * PAIR - 1)], tap_send, tap_recv)


def closing_kernel(own, taps, *refs):
    sources, shared_ref, parts, targets = refs[:4], refs[4], refs[5:7], refs[7:11]
    taps_ref, finals = refs[11], refs[12:]
    for source, target in zip(sources, targets):
        target[0] = source[...].reshape(target.shape[1:])
    for part, final in zip(parts, finals):
        final[...] = part[...]
    rows = shared_ref.shape[1]
    group = lax.broadcasted_iota(jnp.int32, (rows, LANES), 1) // own
    groups = LANES // own
    for b in range(taps_ref.shape[2] // LANES):
        y, pair = b // WIDE, b % WIDE
        value = jnp.zeros((rows, LANES), F32)
        for spot in range(groups):
            z, x = pair * (groups // WIDE) + spot // WIDE, spot % WIDE
            first = (y * WIDE + x) * PAIR
            held = shared_ref[first] + shared_ref[first + 1]
            held = pltpu.roll(held, (spot - z) * own % LANES, 1)
            value = jnp.where(group == spot, held, value)
        for stream in range(3):
            taps_ref[stream, :, pl.ds(b * LANES, LANES)] = value[stream * taps : (stream + 1) * taps]


def per_device(queries, key_stream, value_stream, cotangent, short_taps, residues, decay_rates):
    channels, steps = queries.shape[1], queries.shape[2]
    own, modes = residues.shape
    taps = short_taps.shape[1]
    owners, doubles = lax.axis_size("context"), lax.axis_size("dp")
    scale = 1.0 / math.sqrt(queries.shape[0] * doubles * steps * owners)
    view = (owners // (TALL * WIDE), TALL, WIDE, own, steps)
    wide = jax.ShapeDtypeStruct(view, BF16)
    mode_shape = jax.ShapeDtypeStruct(residues.shape, F32)
    line, reach = steps * SUBS, taps - 1
    vm = pltpu.VMEM
    here = pl.BlockSpec(memory_space=vm)
    away = pl.BlockSpec(memory_space=pl.ANY)
    dma = pltpu.SemaphoreType.DMA
    tap_rows = 3 * taps
    ends = modes // WIDE * SUBS
    streams = [x.reshape(view) for x in (queries, key_stream, value_stream, cotangent)]
    results = pl.pallas_call(
        functools.partial(operator_kernel, modes, taps, steps, doubles, scale),
        out_shape=[vm(view, BF16)] * 4 + [vm((PLANE * PAIR, tap_rows, LANES), F32), vm(residues.shape, F32), vm(residues.shape, F32)],
        in_specs=[away] * 4 + [here] * 3,
        out_specs=[here] * 7,
        scratch_shapes=[vm((PLANE, TALL, own, steps), BF16)] * 8
        + [vm((line + reach * SUBS, LANES), F32)] * 4
        + [vm((line, LANES), F32)] * 7
        + [vm((line + reach * SUBS, LANES), F32)] * 3
        + [
            vm(((2 * modes + 3 * taps) * SUBS, LANES), F32),
            vm((modes * SUBS, LANES), F32),
            vm((modes * SUBS, LANES), F32),
            vm((modes * SUBS, LANES), F32),
            vm((line * modes, LANES), F32),
            vm((modes, LANES), F32),
            vm((modes, LANES), F32),
            vm((tap_rows, LANES), F32),
            vm((2 * modes, LANES), F32),
            vm((TALL, 2 * modes, LANES), F32),
            vm((ends, LANES), F32),
            vm((TALL, ends, LANES), F32),
            vm((ends, LANES), F32),
            vm((TALL, ends, LANES), F32),
            vm((3, reach * SUBS, LANES), F32),
            vm((3, reach * SUBS, LANES), F32),
            vm((tap_rows, LANES), F32),
            vm((TALL * PAIR, tap_rows, LANES), F32),
            vm((modes, LANES), F32),
            vm((TALL, modes, LANES), F32),
            vm((modes, LANES), F32),
            vm((TALL, modes, LANES), F32),
            vm((doubles + 1, 2 * modes, LANES), F32),
            vm((tap_rows, LANES), F32),
        ]
        + [dma((4,))] * 4
        + [dma((16,)), dma((doubles,)), dma((doubles,))]
        + [dma((3,))] * 4
        + [dma((6,))] * 2
        + [dma, dma],
        compiler_params=pltpu.CompilerParams(collective_id=0, has_side_effects=True, vmem_limit_bytes=58 * 1024 * 1024),
    )(*streams, short_taps, residues, decay_rates)
    return pl.pallas_call(
        functools.partial(closing_kernel, own, taps),
        out_shape=[jax.ShapeDtypeStruct(queries.shape, BF16)] * 4
        + [jax.ShapeDtypeStruct(short_taps.shape, F32), mode_shape, mode_shape],
        in_specs=[here] * 7,
        out_specs=[here] * 7,
        compiler_params=pltpu.CompilerParams(vmem_limit_bytes=16 * 1024 * 1024),
    )(*results)


def solution(mesh):
    stream = P("dp", None, "context")
    in_specs = (stream,) * 4 + (P(), P("context", None), P("context", None))
    out_specs = (stream,) * 4 + (P(), P("context", None), P("context", None))
    return jax.shard_map(per_device, mesh=mesh, in_specs=in_specs, out_specs=out_specs, check_vma=False)
```
